128 devices in a mesh: row: 16 (over z_lo, y, core), col: 8 (over x, z_hi).
Axes of the slice: x: 4, y: 4, z: 4 (z_hi: 2, z_lo: 2; z = z_hi * 2 + z_lo), core: 2. Of those that a mesh axis runs over, the one named last changes fastest.
Arguments:
- fixed_matrix_encodings: int32 [8192, 53248], P('row', 'col'), may hold values from 0 to 254, as said below
- line_restore_multiplier: float32 [8192], P('row'), may hold values from 0.001 to 0.01
- central_up_matrix: float32 [8192, 16], P('row', 'col'), may hold values from -1.5 to 1.5
- central_down_matrix: float32 [16, 53248], P('row', 'col'), may hold values from -1.5 to 1.5
- running_mean_up: float32 [8192, 16], P('row', 'col'), may hold values from -1.8 to 1.8
- squared_average_up: float32 [8192, 16], P('row', 'col'), may hold values from 0.05 to 0.5
- running_mean_down: float32 [16, 53248], P('row', 'col'), may hold values from -1.8 to 1.8
- squared_average_down: float32 [16, 53248], P('row', 'col'), may hold values from 0.05 to 0.5
- participant_change_up: bfloat16 [128, 8192, 16], P(('row', 'col')), may hold values from -192 to 192
- participant_change_down: bfloat16 [128, 16, 53248], P(('row', 'col')), may hold values from -192 to 192
- client_tallies: int32 [128, 2], P(('row', 'col')), may hold values from 1 to 64
Outputs:
- combined_normalized_entries: bfloat16 [8192, 53248], P('row', 'col')
- fresh_line_multipliers: float32 [8192], P('row')
- lora_b_next: float32 [8192, 16], P('row', 'col')
- lora_a_next: float32 [16, 53248], P('row', 'col')
- moment_b_next: float32 [8192, 16], P('row', 'col')
- second_b_next: float32 [8192, 16], P('row', 'col')
- moment_a_next: float32 [16, 53248], P('row', 'col')
- second_a_next: float32 [16, 53248], P('row', 'col')
The draws below stay inside these ranges and needn't reach their ends.
Inputs may be any that keep to these rules, and one draw needn't show every extreme that they name: `fixed_matrix_encodings`: FP8 e4m3 bit patterns; the not-a-number patterns 127 and 255 never occur.
All inputs are finite; a program needn't handle non-finite values. Where the reference program divides by a largest or mean magnitude, that divisor is 1e-20 or more.
Results may differ from the reference program's by a relative error of at most 0.0053.
Values may be sent and summed in bfloat16 or wider, within the bound.
No kernel may reach another device: no remote copies, remote signals or barrier semaphores. Data moves between devices by JAX's collectives and lax.ppermute only.
A program may use at most 128 MiB of HBM per device.

```python
import math
import jax
import jax.numpy as jnp
from jax import lax

EMBED_SPAN = 8192
INNER_NEURONS = 53248
ADAPT_DIMENSION = 16
PARTICIPANTS = 128


def draw_fixed_matrix_encodings(key, part):
    raw = jax.random.randint(key, (EMBED_SPAN, INNER_NEURONS), 0, 254)
    return raw + (raw >= 127).astype(jnp.int32)


def draw_client_tallies(key, part):
    base = jax.random.randint(key, (PARTICIPANTS, 2), 1, 23)
    ramp = 42 * jnp.arange(PARTICIPANTS, dtype=jnp.int32) // max(PARTICIPANTS - 1, 1)
    return base + ramp[:, None]


def spiked(drawn, stream_key, source, target, shards_of, factor):
    def block_of(axis_at):
        return (jnp.arange(drawn.shape[axis_at]) // (drawn.shape[axis_at] // shards_of)).reshape((-1,) + (1,) * (drawn.ndim - 1 - axis_at))

    one_side = jax.random.permutation(stream_key, shards_of)[block_of(target)]
    other_side = (block_of(target) + shards_of // 2) % shards_of
    return jnp.where((block_of(source) == one_side) | (block_of(source) == other_side), factor * drawn, drawn)


def block_scale(key, extent, cuts, smallest, high):
    def one(position, blocks):
        heights = jax.random.uniform(jax.random.fold_in(jax.random.fold_in(key, 6), position), (blocks,), jnp.float32, smallest / len(cuts), high / len(cuts))
        return jnp.repeat(jnp.exp(heights), extent[position] // blocks).reshape((-1,) + (1,) * (len(extent) - position - 1))

    factor_of = one(*cuts[0])
    for cut in cuts[1:]:
        factor_of = factor_of * one(*cut)
    return factor_of


def scatter_about(own_key, shape, spread, limit, shards=(), kind=jnp.bfloat16):
    drawn = spread * jax.random.normal(own_key, shape, jnp.float32)
    if shards:
        drawn = drawn * block_scale(own_key, shape, shards, -0.22, 0.18)
    return jnp.clip(drawn, -limit, limit).astype(kind)


def bell_draw_with(key, extent, width, reach, split, heavy, kind=jnp.bfloat16):
    values = width * jax.random.normal(key, extent, jnp.float32)
    if split:
        values = values * block_scale(key, extent, split, -0.22, 0.18)
    return jnp.clip(spiked(values, jax.random.fold_in(key, 3), *heavy), -reach, reach).astype(kind)


def setup_inputs(seed: int = 0) -> dict:
    splits = jax.random.split(jax.random.key(seed), 12)
    return {
        "fixed_matrix_encodings": draw_fixed_matrix_encodings(jax.random.fold_in(splits[11], 71), 0),
        "line_restore_multiplier": jnp.clip(jnp.exp(math.log(0.01) - 2.30258502 * jax.random.uniform(splits[1], (EMBED_SPAN,), jnp.float32) ** block_scale(splits[1], (EMBED_SPAN,), ((0, 16),), -0.2, 0.2)), 0.001, 0.01),
        "central_up_matrix": scatter_about(splits[2], (EMBED_SPAN, ADAPT_DIMENSION), 0.25, 1.5, ((0, 16), (1, 8)), jnp.float32),
        "central_down_matrix": scatter_about(splits[3], (ADAPT_DIMENSION, INNER_NEURONS), 0.25, 1.5, ((0, 16), (1, 8)), jnp.float32),
        "running_mean_up": scatter_about(splits[4], (EMBED_SPAN, ADAPT_DIMENSION), 0.3, 1.8, ((0, 16), (1, 8)), jnp.float32),
        "squared_average_up": jnp.clip(jnp.exp(math.log(0.5) - 2.3025851 * jax.random.uniform(splits[5], (EMBED_SPAN, ADAPT_DIMENSION), jnp.float32) ** block_scale(splits[5], (EMBED_SPAN, ADAPT_DIMENSION), ((0, 16), (1, 8)), -0.2, 0.2)), 0.05, 0.5),
        "running_mean_down": scatter_about(splits[6], (ADAPT_DIMENSION, INNER_NEURONS), 0.3, 1.8, ((0, 16), (1, 8)), jnp.float32),
        "squared_average_down": jnp.clip(jnp.exp(math.log(0.5) - 2.3025851 * jax.random.uniform(splits[7], (ADAPT_DIMENSION, INNER_NEURONS), jnp.float32) ** block_scale(splits[7], (ADAPT_DIMENSION, INNER_NEURONS), ((0, 16), (1, 8)), -0.2, 0.2)), 0.05, 0.5),
        "participant_change_up": bell_draw_with(splits[8], (PARTICIPANTS, EMBED_SPAN, ADAPT_DIMENSION), 8.0, 192.0, ((0, 128),), (0, 1, 128, 5.5)),
        "participant_change_down": bell_draw_with(splits[9], (PARTICIPANTS, ADAPT_DIMENSION, INNER_NEURONS), 8.0, 192.0, ((0, 128),), (0, 2, 128, 5.5)),
        "client_tallies": draw_client_tallies(jax.random.fold_in(splits[11], 71), 0),
    }


first_decay = 0.9
second_decay = 0.99
server_rate = 0.1
adam_floor = 0.001
adapter_scale = 2.0
count_scale = 64.0
fp8_top = 448.0
peak_eps = 1e-06

def decode(codes):
    sign_bit = codes // 128
    exponent = codes // 8 % 16
    mantissa = codes % 8
    gaussian_sample = (8 + mantissa).astype(jnp.float32) * jnp.exp2((exponent - 10).astype(jnp.float32))
    subnormal = mantissa.astype(jnp.float32) * 2.0 ** (-9)
    magnitude = jnp.where(exponent > 0, gaussian_sample, subnormal)
    return magnitude * (1.0 - 2.0 * sign_bit.astype(jnp.float32))

def adaptive_update(param, moment, second, grad):
    moment_next = first_decay * moment + (1.0 - first_decay) * grad
    second_next = second_decay * second + (1.0 - second_decay) * grad * grad
    param_next = param - server_rate * moment_next / (jnp.sqrt(second_next) + adam_floor)
    return (param_next, moment_next, second_next)

def reference(fixed_matrix_encodings, line_restore_multiplier, central_up_matrix, central_down_matrix, running_mean_up, squared_average_up, running_mean_down, squared_average_down, participant_change_up, participant_change_down, client_tallies):
    weights = client_tallies.astype(jnp.float32) / (count_scale * PARTICIPANTS)
    gradient_b = lax.optimization_barrier(jnp.sum(weights[:, 0, None, None] * participant_change_up.astype(jnp.float32), axis=0))
    gradient_a = lax.optimization_barrier(jnp.sum(weights[:, 1, None, None] * participant_change_down.astype(jnp.float32), axis=0))
    updated_factor_b, updated_moment_b, updated_variance_b = adaptive_update(central_up_matrix, running_mean_up, squared_average_up, gradient_b)
    updated_factor_a, updated_moment_a, updated_variance_a = adaptive_update(central_down_matrix, running_mean_down, squared_average_down, gradient_a)
    thin_up_matrix = updated_factor_b.astype(jnp.bfloat16)
    lowrank_a = updated_factor_a.astype(jnp.bfloat16)
    tile_lines = math.gcd(EMBED_SPAN, 512)
    partition_list = EMBED_SPAN // tile_lines

    def submatrix_piece(pieces):
        codes, scales, left_product = pieces
        decode_weight = decode(codes) * scales[:, None]
        merged_weight = decode_weight + adapter_scale * jnp.dot(left_product, lowrank_a, preferred_element_type=jnp.float32)
        peak = lax.optimization_barrier(jnp.max(jnp.abs(merged_weight), axis=1)) + peak_eps
        return ((merged_weight / peak[:, None]).astype(jnp.bfloat16), peak / fp8_top)
    combined_normalized_entries, fresh_line_multipliers = lax.map(submatrix_piece, (fixed_matrix_encodings.reshape(partition_list, tile_lines, INNER_NEURONS), line_restore_multiplier.reshape(partition_list, tile_lines), thin_up_matrix.reshape(partition_list, tile_lines, ADAPT_DIMENSION)))
    return (combined_normalized_entries.reshape(EMBED_SPAN, INNER_NEURONS), fresh_line_multipliers.reshape(EMBED_SPAN), updated_factor_b, updated_factor_a, updated_moment_b, updated_variance_b, updated_moment_a, updated_variance_a)
```

```python
import functools

import jax
import jax.numpy as jnp
from jax import lax
from jax.experimental import pallas as pl
from jax.experimental.pallas import tpu as pltpu
from jax.sharding import Mesh, PartitionSpec as P

first_decay = 0.9
second_decay = 0.99
server_rate = 0.1
adam_floor = 0.001
adapter_scale = 2.0
count_scale = 64.0
fp8_top = 448.0
peak_eps = 1e-06

f32, bf16, i32 = jnp.float32, jnp.bfloat16, jnp.int32
SDS = jax.ShapeDtypeStruct

ROW, COL = ("zl", "y", "c"), ("x", "zh")
CHIPS, COLS = 8, 8
RANKS = 16
DEPTH, WIDTH = 512, 6656
HALF = WIDTH // 2
FULL_B, FULL_A = DEPTH * 16, WIDTH * 8
LANES = HALF + DEPTH
PIECE = 512
PIECES = WIDTH // PIECE


def adaptive_update(param, moment, second, grad):
    moment_next = first_decay * moment + (1.0 - first_decay) * grad
    second_next = second_decay * second + (1.0 - second_decay) * grad * grad
    param_next = param - server_rate * moment_next / (jnp.sqrt(second_next) + adam_floor)
    return (param_next, moment_next, second_next)


def params_for(mib):
    return pltpu.CompilerParams(vmem_limit_bytes=mib << 20)


def in_hbm():
    return pl.BlockSpec(memory_space=pltpu.HBM)


def stay(x):
    return pltpu.with_memory_space_constraint(x, pltpu.HBM)


def near(x):
    return pltpu.with_memory_space_constraint(x, pltpu.VMEM)


def in_any():
    return pl.BlockSpec(memory_space=pl.ANY)


def in_vmem():
    return pl.BlockSpec(memory_space=pltpu.VMEM)


def in_smem():
    return pl.BlockSpec(memory_space=pltpu.SMEM)


DEC_ROWS = 32
SLOTS = 3


def decode_kernel(*refs):
    codes, state = refs[0], refs[1:7]
    out, kept = refs[7], refs[8:14]
    buf, done, sems, out_sems, state_sems = refs[14:]
    steps = DEPTH // DEC_ROWS

    def rows(step):
        return pl.ds(pl.multiple_of(step * DEC_ROWS, DEC_ROWS), DEC_ROWS)

    def fetch(step, slot):
        return pltpu.make_async_copy(codes.at[rows(step), :], buf.at[slot], sems.at[slot])

    def store(step, slot):
        return pltpu.make_async_copy(done.at[slot], out.at[rows(step), :], out_sems.at[slot])

    for s in range(SLOTS - 1):
        fetch(s, s).start()
    moves = [pltpu.make_async_copy(a, b, state_sems.at[q]) for q, (a, b) in enumerate(zip(state, kept))]
    for move in moves:
        move.start()

    def step(s, carry):
        slot = lax.rem(s, SLOTS)
        fetch(s, slot).wait()

        @pl.when(s + SLOTS - 1 < steps)
        def _():
            fetch(s + SLOTS - 1, lax.rem(s + SLOTS - 1, SLOTS)).start()

        @pl.when(s >= SLOTS)
        def _():
            store(s - SLOTS, slot).wait()

        def group(g, carry):
            at = pl.ds(pl.multiple_of(g * 16, 16), 16)
            for t in range(PIECES):
                here = pl.ds(t * PIECE, PIECE)
                code = buf[slot, at, here]
                exponent = jnp.bitwise_and(lax.shift_right_logical(code, 3), 15)
                mantissa = jnp.bitwise_and(code, 7)
                whole = jnp.where(exponent > 0, mantissa + 8, mantissa)
                value = lax.shift_left(whole, jnp.maximum(exponent, 1))
                value = jnp.where(code >= 128, -value, value)
                done[slot, at, here] = value.astype(f32).astype(bf16)
            return carry

        lax.fori_loop(0, DEC_ROWS // 16, group, 0)
        store(s, slot).start()
        return carry

    lax.fori_loop(0, steps, step, 0)
    for s in range(steps - SLOTS, steps):
        store(s, s % SLOTS).wait()
    for move in moves:
        move.wait()


def decode(codes, state):
    return pl.pallas_call(
        decode_kernel,
        out_shape=(pltpu.HBM((DEPTH, WIDTH), bf16),) + tuple(pltpu.VMEM(x.shape, f32) for x in state),
        in_specs=[in_hbm()] * 7,
        out_specs=(in_hbm(),) + (in_vmem(),) * 6,
        scratch_shapes=[
            pltpu.VMEM((SLOTS, DEC_ROWS, WIDTH), i32),
            pltpu.VMEM((SLOTS, DEC_ROWS, WIDTH), bf16),
            pltpu.SemaphoreType.DMA((SLOTS,)),
            pltpu.SemaphoreType.DMA((SLOTS,)),
            pltpu.SemaphoreType.DMA((6,)),
        ],
        compiler_params=params_for(8),
        cost_estimate=pl.CostEstimate(flops=40_000_000, transcendentals=0, bytes_accessed=24_000_000),
        name="decode",
    )(stay(codes), *[stay(x) for x in state])


def pair_kernel(own_w, mate_w, own_a, mate_a, own_b, mate_b, out, xa, xb, sem_a, sem_b):
    core = lax.axis_index("c")
    part = HALF // 2
    copies = {}
    for t in range(2):
        for src, ref in enumerate((own_a, mate_a)):
            for c in range(COLS):
                start = pl.multiple_of(c * WIDTH + core * HALF + t * part, 128)
                copies[t, src, c] = pltpu.make_async_copy(
                    ref.at[:, pl.ds(start, part)],
                    xa.at[pl.ds(src * 128 + c * 16, 16), pl.ds(t * part, part)],
                    sem_a.at[t, src, c],
                )
                copies[t, src, c].start()
        if t == 0:
            b_copies = []
            for src, ref in enumerate((own_b, mate_b)):
                b_copies.append(
                    pltpu.make_async_copy(
                        ref.at[pl.ds(pl.multiple_of(core * 8, 8), 8), :], xb.at[src], sem_b.at[src]
                    )
                )
                b_copies[-1].start()
    o = lax.broadcasted_iota(i32, (128, 256), 0)
    k = lax.broadcasted_iota(i32, (128, 256), 1)
    same_block = jnp.bitwise_and(lax.shift_right_logical(o, 1), 7) == jnp.bitwise_and(
        lax.shift_right_logical(k, 4), 7
    )
    rank = lax.shift_right_logical(o, 4) * 2 + jnp.bitwise_and(o, 1)
    same_rank = rank == jnp.bitwise_and(k, 15)
    weight = jnp.where(k < 128, own_w[0, 1], mate_w[0, 1])
    pick = jnp.where(jnp.logical_and(same_block, same_rank), weight, 0.0).astype(bf16)
    for b in b_copies:
        b.wait()
    for j in range(CHIPS):
        halves = []
        for p in range(2):
            at = pl.ds((2 * j + p) * DEPTH, DEPTH)
            halves.append(
                own_w[0, 0] * xb[0, :, at].astype(f32) + mate_w[0, 0] * xb[1, :, at].astype(f32)
            )
        out[pl.ds(j * 16, 16), pl.ds(HALF, DEPTH)] = jnp.concatenate(halves, axis=0).astype(bf16)
    for t in range(2):
        for src in range(2):
            for c in range(COLS):
                copies[t, src, c].wait()
        at = pl.ds(t * part, part)
        out[:, at] = jnp.dot(pick, xa[:, at], preferred_element_type=f32).astype(bf16)


def pair_sum(own_w, mate_w, own_a, mate_a, own_b, mate_b):
    return pl.pallas_call(
        pair_kernel,
        out_shape=SDS((CHIPS * 16, LANES), bf16),
        in_specs=[in_smem(), in_smem(), in_hbm(), in_any(), in_hbm(), in_any()],
        out_specs=in_vmem(),
        scratch_shapes=[
            pltpu.VMEM((256, HALF), bf16),
            pltpu.VMEM((2, 8, FULL_B), bf16),
            pltpu.SemaphoreType.DMA((2, 2, COLS)),
            pltpu.SemaphoreType.DMA((2,)),
        ],
        compiler_params=params_for(16),
        name="pair_sum",
    )(own_w, mate_w, stay(own_a), mate_a, stay(own_b), mate_b)


def row_kernel(got, out, scr):
    total = got[0].astype(f32)
    for j in range(1, CHIPS):
        total = total + got[j].astype(f32)
    scr[...] = jnp.zeros_like(scr)
    for d in range(16):
        core, col = divmod(d, COLS)
        a = 2 * col + core
        for i in range(7):
            w = min(PIECE, HALF - i * PIECE)
            scr[d, pl.ds(i, 1), pl.ds(0, w)] = total[a : a + 1, i * PIECE : i * PIECE + w]
        scr[d, pl.ds(8, 8), :] = total[core * 8 : core * 8 + 8, HALF:LANES]
    out[...] = scr[...].astype(bf16)


def row_sum(got):
    return pl.pallas_call(
        row_kernel,
        out_shape=SDS((16, 16, PIECE), bf16),
        in_specs=[in_vmem()],
        out_specs=in_vmem(),
        scratch_shapes=[pltpu.VMEM((16, 16, PIECE), f32)],
        compiler_params=params_for(16),
        name="row_sum",
    )(got)


APART = (0, 1, 4, 5, 2, 3, 6, 7)


def col_gather(block):
    for axis, perm in (
        ("zh", [(0, 1), (1, 0)]),
        ("x", [(0, 2), (1, 3), (2, 0), (3, 1)]),
        ("x", [(0, 1), (1, 0), (2, 3), (3, 2)]),
    ):
        other = lax.ppermute(block, axis, perm)
        last, block = block, jnp.concatenate([block, other], axis=0)
    return last, other


def step_kernel(
    got, state_0, state_1, pa, ma, va, pb, mb, vb,
    pa_n, ma_n, va_n, pb_n, mb_n, vb_n, send, factor, ga, scr, rows,
):
    col = lax.axis_index("x") * 2 + lax.axis_index("zh")
    tops = []
    for h in range(2):
        acc = got[h * 8, 0:16, :].astype(f32)
        for c in range(1, COLS):
            acc = acc + got[h * 8 + c, 0:16, :].astype(f32)
        for i in range(7):
            w = min(PIECE, HALF - i * PIECE)
            ga[:, pl.ds(h * HALF + i * PIECE, w)] = acc[i : i + 1, 0:w]
        tops.append(acc[8:16, :])
    gb = jnp.concatenate(tops, axis=0)
    for n, apart in enumerate(APART):
        block = (state_0, state_1)[n // 4][pl.ds(n % 4 * 8, 8), :]
        owner = jnp.bitwise_xor(col, apart)
        for q in range(3):
            scr[q, owner] = block[2 * q : 2 * q + 2, :]
    whole = [scr[q].reshape(RANKS, DEPTH) for q in range(3)]
    full = adaptive_update(*whole, gb)[0]
    factor[...] = full.astype(bf16)
    at = lax.broadcasted_iota(i32, gb.shape, 0)
    own = [
        jnp.sum(jnp.where(at == 2 * col + q, gb, 0.0), axis=0, keepdims=True) for q in range(2)
    ]
    pb_n[...], mb_n[...], vb_n[...] = adaptive_update(
        pb[...], mb[...], vb[...], jnp.concatenate(own, axis=0)
    )
    pn, mn, vn = adaptive_update(pa[...], ma[...], va[...], ga[...])
    pa_n[...], ma_n[...], va_n[...] = pn, mn, vn
    rows[...] = jnp.zeros_like(rows)
    for i in range(PIECES):
        rows[pl.ds(i, 1), :] = pn[:, i * PIECE : (i + 1) * PIECE]
    message = rows[...].astype(bf16)
    for d in range(16):
        send[d] = message


def server_step(got, col_state, a_state, b_state):
    a_shape, b_shape = SDS((1, WIDTH), f32), SDS((2, DEPTH), f32)
    return pl.pallas_call(
        step_kernel,
        out_shape=(a_shape,) * 3
        + (b_shape,) * 3
        + (SDS((16, 16, PIECE), bf16), SDS((RANKS, DEPTH), bf16)),
        in_specs=[in_vmem()] * 9,
        out_specs=(in_vmem(),) * 8,
        scratch_shapes=[
            pltpu.VMEM((1, WIDTH), f32),
            pltpu.VMEM((3, COLS, 2, DEPTH), f32),
            pltpu.VMEM((16, PIECE), f32),
        ],
        compiler_params=params_for(16),
        name="server_step",
    )(got, *col_state, *map(near, a_state), *map(near, b_state))


def spread_kernel(factor, out):
    k = lax.broadcasted_iota(i32, (RANKS, 256), 1)
    r = lax.broadcasted_iota(i32, (RANKS, 256), 0)
    repeat = jnp.where(lax.shift_right_logical(k, 4) == r, adapter_scale, 0.0).astype(bf16)
    tall = jnp.transpose(factor[...].astype(f32)).astype(bf16)
    out[...] = jnp.dot(tall, repeat, preferred_element_type=f32).astype(bf16)


def spread(factor):
    return pl.pallas_call(
        spread_kernel,
        out_shape=SDS((DEPTH, 256), bf16),
        in_specs=[in_vmem()],
        out_specs=in_vmem(),
        compiler_params=params_for(16),
        name="spread",
    )(factor)


BLOCK = 512


def merge_kernel(dec, scale, wide, ranks, merged, peaks, buf, row_scale, tops, sems):
    fetches = []
    for i in range(PIECES):
        fetches.append(
            pltpu.make_async_copy(dec.at[:, pl.ds(i * PIECE, PIECE)], buf.at[i], sems.at[i])
        )
        fetches[-1].start()
    row_scale[...] = jnp.transpose(jnp.broadcast_to(scale[...] * 2.0**-10, (128, DEPTH)))
    lane = jnp.bitwise_and(lax.broadcasted_iota(i32, (BLOCK, 256), 1), 15)
    right = ranks[...].reshape(256, PIECE)
    tops[...] = jnp.zeros_like(tops)
    for i in range(PIECES):
        fetches[i].wait()
        for b in range(DEPTH // BLOCK):
            at = pl.ds(b * BLOCK, BLOCK)
            left = wide[at, :]
            one = jnp.where(lane == i, left, jnp.zeros_like(left))
            low = jnp.dot(one, right, preferred_element_type=f32)
            top = tops[at, :]
            for t in range(PIECE // 128):
                here = pl.ds(t * 128, 128)
                whole = buf[i, at, here].astype(f32) * row_scale[at, :] + low[:, t * 128 : t * 128 + 128]
                merged[i, at, here] = whole
                top = jnp.maximum(top, jnp.abs(whole))
            tops[at, :] = top
    peak = jnp.max(jnp.transpose(tops[...]), axis=0, keepdims=True)
    for c in range(COLS):
        peaks[c] = peak


def merge(dec, scale, wide, ranks):
    return pl.pallas_call(
        merge_kernel,
        out_shape=(pltpu.VMEM((PIECES, DEPTH, PIECE), f32), SDS((COLS, 1, DEPTH), f32)),
        in_specs=[in_hbm()] + [in_vmem()] * 3,
        out_specs=(in_vmem(), in_vmem()),
        scratch_shapes=[
            pltpu.VMEM((PIECES, DEPTH, PIECE), bf16),
            pltpu.VMEM((DEPTH, 128), f32),
            pltpu.VMEM((DEPTH, 128), f32),
            pltpu.SemaphoreType.DMA((PIECES,)),
        ],
        compiler_params=params_for(16),
        name="merge",
    )(stay(dec), scale, wide, ranks)


OUT_ROWS = 32


def normalise_kernel(merged, peaks, out, scales, inverse, buf, sems):
    peak = peaks[0]
    for c in range(1, COLS):
        peak = jnp.maximum(peak, peaks[c])
    peak = peak + peak_eps
    scales[...] = peak / fp8_top
    inverse[...] = jnp.transpose(jnp.broadcast_to(1.0 / peak, (128, DEPTH)))
    steps, slots = DEPTH // OUT_ROWS, 4

    def store(step, slot):
        return pltpu.make_async_copy(
            buf.at[slot],
            out.at[pl.ds(pl.multiple_of(step * OUT_ROWS, OUT_ROWS), OUT_ROWS), :],
            sems.at[slot],
        )

    def step(s, carry):
        slot = lax.rem(s, slots)

        @pl.when(s >= slots)
        def _():
            store(s - slots, slot).wait()

        for g in range(OUT_ROWS // 16):
            row = pl.multiple_of(s * OUT_ROWS + g * 16, 16)
            inv = inverse[pl.ds(row, 16), :]
            inv = jnp.concatenate([inv] * (PIECE // 128), axis=1)
            for t in range(PIECES):
                here = pl.ds(t * PIECE, PIECE)
                buf[slot, pl.ds(g * 16, 16), here] = (merged[t, pl.ds(row, 16), :] * inv).astype(bf16)
        store(s, slot).start()
        return carry

    lax.fori_loop(0, steps, step, 0)
    for s in range(steps - slots, steps):
        store(s, s % slots).wait()


def normalise(merged, peaks):
    return pl.pallas_call(
        normalise_kernel,
        out_shape=(SDS((DEPTH, WIDTH), bf16), SDS((1, DEPTH), f32)),
        in_specs=[in_vmem(), in_vmem()],
        out_specs=(in_hbm(), in_vmem()),
        scratch_shapes=[
            pltpu.VMEM((DEPTH, 128), f32),
            pltpu.VMEM((4, OUT_ROWS, WIDTH), bf16),
            pltpu.SemaphoreType.DMA((4,)),
        ],
        compiler_params=params_for(16),
        name="normalise",
    )(near(merged), peaks)


def local(codes, scale, pb, pa, mb, vb, ma, va, delta_b, delta_a, tallies):
    exchange = functools.partial(lax.all_to_all, split_axis=0, concat_axis=0, tiled=True)
    mate = functools.partial(lax.ppermute, axis_name="c", perm=[(0, 1), (1, 0)])
    weights = tallies.astype(f32) / (count_scale * 128)
    own_a = delta_a.reshape(RANKS, FULL_A)
    own_b = delta_b.reshape(FULL_B, RANKS).T
    mate_a, mate_b, mate_w = mate(own_a), mate(own_b), mate(weights)
    pb, mb, vb = pb.T, mb.T, vb.T
    col_state = col_gather(jnp.concatenate([pb, mb, vb, pb], axis=0))
    pairs = pair_sum(weights, mate_w, own_a, mate_a, own_b, mate_b)
    got = exchange(pairs.reshape(CHIPS, 16, LANES), ("zl", "y"))
    got, col_state = lax.optimization_barrier((got, col_state))
    message = row_sum(got)
    codes, message = lax.optimization_barrier((codes, message))
    dec, *state = decode(codes, (pa, ma, va, pb, mb, vb))
    got = exchange(message, ("c",) + COL)
    pa_n, ma_n, va_n, pb_n, mb_n, vb_n, send, factor = server_step(
        got, col_state, state[:3], state[3:]
    )
    ranks = exchange(send, ROW)
    merged, peaks = merge(dec, scale.reshape(1, DEPTH), spread(factor), ranks)
    out, scales = normalise(merged, exchange(peaks, COL))
    return (out, scales.reshape(DEPTH), pb_n.T, pa_n, mb_n.T, vb_n.T, ma_n, va_n)


def solution(mesh):
    split = Mesh(mesh.devices.reshape(2, 4, 2, 4, 2), ROW + COL)
    tile, everyone = P(ROW, COL), P(ROW + COL, None, None)
    return jax.shard_map(
        local,
        mesh=split,
        in_specs=(tile, P(ROW)) + (tile,) * 6 + (everyone, everyone, P(ROW + COL, None)),
        out_specs=(tile, P(ROW)) + (tile,) * 6,
        check_vma=False,
    )
```

```python
import functools

import jax
import jax.numpy as jnp
from jax import lax
from jax.experimental import pallas as pl
from jax.experimental.pallas import tpu as pltpu
from jax.sharding import Mesh, PartitionSpec as P

first_decay = 0.9
second_decay = 0.99
server_rate = 0.1
adam_floor = 0.001
adapter_scale = 2.0
count_scale = 64.0
fp8_top = 448.0
peak_eps = 1e-06

f32, bf16, i32 = jnp.float32, jnp.bfloat16, jnp.int32
SDS = jax.ShapeDtypeStruct

ROW, COL = ("zl", "y", "c"), ("x", "zh")
CHIPS, COLS = 8, 8
RANKS = 16
DEPTH, WIDTH = 512, 6656
HALF = WIDTH // 2
FULL_B, FULL_A = DEPTH * 16, WIDTH * 8
LANES = HALF + DEPTH
PIECE = 512
PIECES = WIDTH // PIECE


def adaptive_update(param, moment, second, grad):
    moment_next = first_decay * moment + (1.0 - first_decay) * grad
    second_next = second_decay * second + (1.0 - second_decay) * grad * grad
    param_next = param - server_rate * moment_next / (jnp.sqrt(second_next) + adam_floor)
    return (param_next, moment_next, second_next)


def params_for(mib):
    return pltpu.CompilerParams(vmem_limit_bytes=mib << 20)


def in_hbm():
    return pl.BlockSpec(memory_space=pltpu.HBM)


def stay(x):
    return pltpu.with_memory_space_constraint(x, pltpu.HBM)


def near(x):
    return pltpu.with_memory_space_constraint(x, pltpu.VMEM)


def in_any():
    return pl.BlockSpec(memory_space=pl.ANY)


def in_vmem():
    return pl.BlockSpec(memory_space=pltpu.VMEM)


def in_smem():
    return pl.BlockSpec(memory_space=pltpu.SMEM)


DEC_ROWS = 32
SLOTS = 3
PART = DEPTH // 2


def decode_kernel(first, count, *refs):
    codes, state = refs[0], refs[1 : 1 + count]
    out, kept = refs[1 + count], refs[2 + count : 2 + 2 * count]
    buf, done, sems, out_sems, state_sems = refs[2 + 2 * count :]
    steps = PART // DEC_ROWS

    def rows(step):
        return pl.ds(pl.multiple_of(step * DEC_ROWS, DEC_ROWS), DEC_ROWS)

    def fetch(step, slot):
        return pltpu.make_async_copy(
            codes.at[rows(step + first // DEC_ROWS), :], buf.at[slot], sems.at[slot]
        )

    def store(step, slot):
        return pltpu.make_async_copy(done.at[slot], out.at[rows(step), :], out_sems.at[slot])

    for s in range(SLOTS - 1):
        fetch(s, s).start()
    moves = [pltpu.make_async_copy(a, b, state_sems.at[q]) for q, (a, b) in enumerate(zip(state, kept))]
    for move in moves:
        move.start()

    def step(s, carry):
        slot = lax.rem(s, SLOTS)
        fetch(s, slot).wait()

        @pl.when(s + SLOTS - 1 < steps)
        def _():
            fetch(s + SLOTS - 1, lax.rem(s + SLOTS - 1, SLOTS)).start()

        @pl.when(s >= SLOTS)
        def _():
            store(s - SLOTS, slot).wait()

        def group(g, carry):
            at = pl.ds(pl.multiple_of(g * 16, 16), 16)
            for t in range(PIECES):
                here = pl.ds(t * PIECE, PIECE)
                code = buf[slot, at, here]
                exponent = jnp.bitwise_and(lax.shift_right_logical(code, 3), 15)
                mantissa = jnp.bitwise_and(code, 7)
                whole = jnp.where(exponent > 0, mantissa + 8, mantissa)
                value = lax.shift_left(whole, jnp.maximum(exponent, 1))
                value = jnp.where(code >= 128, -value, value)
                done[slot, at, here] = value.astype(f32).astype(bf16)
            return carry

        lax.fori_loop(0, DEC_ROWS // 16, group, 0)
        store(s, slot).start()
        return carry

    lax.fori_loop(0, steps, step, 0)
    for s in range(steps - SLOTS, steps):
        store(s, s % SLOTS).wait()
    for move in moves:
        move.wait()


def decode(codes, first, state=()):
    count = len(state)
    return pl.pallas_call(
        functools.partial(decode_kernel, first, count),
        out_shape=(pltpu.HBM((PART, WIDTH), bf16),) + tuple(pltpu.VMEM(x.shape, f32) for x in state),
        in_specs=[in_hbm()] * (1 + count),
        out_specs=(in_hbm(),) + (in_vmem(),) * count,
        scratch_shapes=[
            pltpu.VMEM((SLOTS, DEC_ROWS, WIDTH), i32),
            pltpu.VMEM((SLOTS, DEC_ROWS, WIDTH), bf16),
            pltpu.SemaphoreType.DMA((SLOTS,)),
            pltpu.SemaphoreType.DMA((SLOTS,)),
            pltpu.SemaphoreType.DMA((6,)),
        ],
        compiler_params=params_for(8),
        cost_estimate=pl.CostEstimate(flops=20_000_000, transcendentals=0, bytes_accessed=12_000_000),
        name="decode",
    )(stay(codes), *[stay(x) for x in state])


def pair_kernel(own_w, mate_w, own_a, mate_a, own_b, mate_b, out, xa, xb, sem_a, sem_b):
    core = lax.axis_index("c")
    part = HALF // 2
    copies = {}
    for t in range(2):
        for src, ref in enumerate((own_a, mate_a)):
            for c in range(COLS):
                start = pl.multiple_of(c * WIDTH + core * HALF + t * part, 128)
                copies[t, src, c] = pltpu.make_async_copy(
                    ref.at[:, pl.ds(start, part)],
                    xa.at[pl.ds(src * 128 + c * 16, 16), pl.ds(t * part, part)],
                    sem_a.at[t, src, c],
                )
                copies[t, src, c].start()
        if t == 0:
            b_copies = []
            for src, ref in enumerate((own_b, mate_b)):
                b_copies.append(
                    pltpu.make_async_copy(
                        ref.at[pl.ds(pl.multiple_of(core * 8, 8), 8), :], xb.at[src], sem_b.at[src]
                    )
                )
                b_copies[-1].start()
    o = lax.broadcasted_iota(i32, (128, 256), 0)
    k = lax.broadcasted_iota(i32, (128, 256), 1)
    same_block = jnp.bitwise_and(lax.shift_right_logical(o, 1), 7) == jnp.bitwise_and(
        lax.shift_right_logical(k, 4), 7
    )
    rank = lax.shift_right_logical(o, 4) * 2 + jnp.bitwise_and(o, 1)
    same_rank = rank == jnp.bitwise_and(k, 15)
    weight = jnp.where(k < 128, own_w[0, 1], mate_w[0, 1])
    pick = jnp.where(jnp.logical_and(same_block, same_rank), weight, 0.0).astype(bf16)
    for b in b_copies:
        b.wait()
    for j in range(CHIPS):
        halves = []
        for p in range(2):
            at = pl.ds((2 * j + p) * DEPTH, DEPTH)
            halves.append(
                own_w[0, 0] * xb[0, :, at].astype(f32) + mate_w[0, 0] * xb[1, :, at].astype(f32)
            )
        out[pl.ds(j * 16, 16), pl.ds(HALF, DEPTH)] = jnp.concatenate(halves, axis=0).astype(bf16)
    for t in range(2):
        for src in range(2):
            for c in range(COLS):
                copies[t, src, c].wait()
        at = pl.ds(t * part, part)
        out[:, at] = jnp.dot(pick, xa[:, at], preferred_element_type=f32).astype(bf16)


def pair_sum(own_w, mate_w, own_a, mate_a, own_b, mate_b):
    return pl.pallas_call(
        pair_kernel,
        out_shape=SDS((CHIPS * 16, LANES), bf16),
        in_specs=[in_smem(), in_smem(), in_hbm(), in_any(), in_hbm(), in_any()],
        out_specs=in_vmem(),
        scratch_shapes=[
            pltpu.VMEM((256, HALF), bf16),
            pltpu.VMEM((2, 8, FULL_B), bf16),
            pltpu.SemaphoreType.DMA((2, 2, COLS)),
            pltpu.SemaphoreType.DMA((2,)),
        ],
        compiler_params=params_for(16),
        name="pair_sum",
    )(own_w, mate_w, stay(own_a), mate_a, stay(own_b), mate_b)


def row_kernel(got, out, scr):
    total = got[0].astype(f32)
    for j in range(1, CHIPS):
        total = total + got[j].astype(f32)
    scr[...] = jnp.zeros_like(scr)
    for d in range(16):
        core, col = divmod(d, COLS)
        a = 2 * col + core
        for i in range(7):
            w = min(PIECE, HALF - i * PIECE)
            scr[d, pl.ds(i, 1), pl.ds(0, w)] = total[a : a + 1, i * PIECE : i * PIECE + w]
        scr[d, pl.ds(8, 8), :] = total[core * 8 : core * 8 + 8, HALF:LANES]
    out[...] = scr[...].astype(bf16)


def row_sum(got):
    return pl.pallas_call(
        row_kernel,
        out_shape=SDS((16, 16, PIECE), bf16),
        in_specs=[in_vmem()],
        out_specs=in_vmem(),
        scratch_shapes=[pltpu.VMEM((16, 16, PIECE), f32)],
        compiler_params=params_for(16),
        name="row_sum",
    )(got)


APART = (0, 1, 4, 5, 2, 3, 6, 7)


def x_gather(block):
    for perm in ([(0, 2), (1, 3), (2, 0), (3, 1)], [(0, 1), (1, 0), (2, 3), (3, 2)]):
        other = lax.ppermute(block, "x", perm)
        last, block = block, jnp.concatenate([block, other], axis=0)
    return last, other


def step_kernel(
    got, state_0, state_1, pa, ma, va, pb, mb, vb,
    pa_n, ma_n, va_n, pb_n, mb_n, vb_n, send, factor, ga, scr, rows,
):
    col = lax.axis_index("x") * 2 + lax.axis_index("zh")
    tops = []
    for h in range(2):
        acc = got[h * 8, 0:16, :].astype(f32)
        for c in range(1, COLS):
            acc = acc + got[h * 8 + c, 0:16, :].astype(f32)
        for i in range(7):
            w = min(PIECE, HALF - i * PIECE)
            ga[:, pl.ds(h * HALF + i * PIECE, w)] = acc[i : i + 1, 0:w]
        tops.append(acc[8:16, :])
    gb = jnp.concatenate(tops, axis=0)
    for n, apart in enumerate(APART):
        block = (state_0, state_1)[n // 4][pl.ds(n % 4 * 8, 8), :]
        owner = jnp.bitwise_xor(col, apart)
        for q in range(3):
            scr[q, owner] = block[2 * q : 2 * q + 2, :]
    whole = [scr[q].reshape(RANKS, DEPTH) for q in range(3)]
    full = adaptive_update(*whole, gb)[0]
    factor[...] = full.astype(bf16)
    at = lax.broadcasted_iota(i32, gb.shape, 0)
    own = [
        jnp.sum(jnp.where(at == 2 * col + q, gb, 0.0), axis=0, keepdims=True) for q in range(2)
    ]
    pb_n[...], mb_n[...], vb_n[...] = adaptive_update(
        pb[...], mb[...], vb[...], jnp.concatenate(own, axis=0)
    )
    pn, mn, vn = adaptive_update(pa[...], ma[...], va[...], ga[...])
    pa_n[...], ma_n[...], va_n[...] = pn, mn, vn
    rows[...] = jnp.zeros_like(rows)
    for i in range(PIECES):
        rows[pl.ds(i, 1), :] = pn[:, i * PIECE : (i + 1) * PIECE]
    message = rows[...].astype(bf16)
    for d in range(16):
        send[d] = message


def server_step(got, col_state, a_state, b_state):
    a_shape, b_shape = SDS((1, WIDTH), f32), SDS((2, DEPTH), f32)
    return pl.pallas_call(
        step_kernel,
        out_shape=(a_shape,) * 3
        + (b_shape,) * 3
        + (SDS((16, 16, PIECE), bf16), SDS((RANKS, DEPTH), bf16)),
        in_specs=[in_vmem()] * 9,
        out_specs=(in_vmem(),) * 8,
        scratch_shapes=[
            pltpu.VMEM((1, WIDTH), f32),
            pltpu.VMEM((3, COLS, 2, DEPTH), f32),
            pltpu.VMEM((16, PIECE), f32),
        ],
        compiler_params=params_for(16),
        name="server_step",
    )(got, *col_state, *map(near, a_state), *map(near, b_state))


def spread_kernel(factor, out):
    k = lax.broadcasted_iota(i32, (RANKS, 256), 1)
    r = lax.broadcasted_iota(i32, (RANKS, 256), 0)
    repeat = jnp.where(lax.shift_right_logical(k, 4) == r, adapter_scale, 0.0).astype(bf16)
    tall = jnp.transpose(factor[...].astype(f32)).astype(bf16)
    out[...] = jnp.dot(tall, repeat, preferred_element_type=f32).astype(bf16)


def spread(factor):
    return pl.pallas_call(
        spread_kernel,
        out_shape=SDS((DEPTH, 256), bf16),
        in_specs=[in_vmem()],
        out_specs=in_vmem(),
        compiler_params=params_for(16),
        name="spread",
    )(factor)


BLOCK = 512


def merge_kernel(dec_top, dec_low, scale, wide, ranks, merged, peaks, buf, row_scale, tops, sems):
    fetches = []
    for i in range(PIECES):
        here = pl.ds(i * PIECE, PIECE)
        fetches.append(
            [
                pltpu.make_async_copy(dec.at[:, here], buf.at[i, pl.ds(q * PART, PART), :], sems.at[i, q])
                for q, dec in enumerate((dec_top, dec_low))
            ]
        )
        for fetch in fetches[-1]:
            fetch.start()
    row_scale[...] = jnp.transpose(jnp.broadcast_to(scale[...] * 2.0**-10, (128, DEPTH)))
    lane = jnp.bitwise_and(lax.broadcasted_iota(i32, (BLOCK, 256), 1), 15)
    right = ranks[...].reshape(256, PIECE)
    tops[...] = jnp.zeros_like(tops)
    for i in range(PIECES):
        for fetch in fetches[i]:
            fetch.wait()
        for b in range(DEPTH // BLOCK):
            at = pl.ds(b * BLOCK, BLOCK)
            left = wide[at, :]
            one = jnp.where(lane == i, left, jnp.zeros_like(left))
            low = jnp.dot(one, right, preferred_element_type=f32)
            top = tops[at, :]
            for t in range(PIECE // 128):
                here = pl.ds(t * 128, 128)
                whole = buf[i, at, here].astype(f32) * row_scale[at, :] + low[:, t * 128 : t * 128 + 128]
                merged[i, at, here] = whole
                top = jnp.maximum(top, jnp.abs(whole))
            tops[at, :] = top
    peak = jnp.max(jnp.transpose(tops[...]), axis=0, keepdims=True)
    for c in range(COLS):
        peaks[c] = peak


def merge(decs, scale, wide, ranks):
    return pl.pallas_call(
        merge_kernel,
        out_shape=(pltpu.VMEM((PIECES, DEPTH, PIECE), f32), SDS((COLS, 1, DEPTH), f32)),
        in_specs=[in_hbm()] * 2 + [in_vmem()] * 3,
        out_specs=(in_vmem(), in_vmem()),
        scratch_shapes=[
            pltpu.VMEM((PIECES, DEPTH, PIECE), bf16),
            pltpu.VMEM((DEPTH, 128), f32),
            pltpu.VMEM((DEPTH, 128), f32),
            pltpu.SemaphoreType.DMA((PIECES, 2)),
        ],
        compiler_params=params_for(16),
        name="merge",
    )(*map(stay, decs), scale, wide, ranks)


OUT_ROWS = 32


def normalise_kernel(merged, peaks, out, scales, inverse, buf, sems):
    peak = peaks[0]
    for c in range(1, COLS):
        peak = jnp.maximum(peak, peaks[c])
    peak = peak + peak_eps
    scales[...] = peak / fp8_top
    inverse[...] = jnp.transpose(jnp.broadcast_to(1.0 / peak, (128, DEPTH)))
    steps, slots = DEPTH // OUT_ROWS, 4

    def store(step, slot):
        return pltpu.make_async_copy(
            buf.at[slot],
            out.at[pl.ds(pl.multiple_of(step * OUT_ROWS, OUT_ROWS), OUT_ROWS), :],
            sems.at[slot],
        )

    def step(s, carry):
        slot = lax.rem(s, slots)

        @pl.when(s >= slots)
        def _():
            store(s - slots, slot).wait()

        for g in range(OUT_ROWS // 16):
            row = pl.multiple_of(s * OUT_ROWS + g * 16, 16)
            inv = inverse[pl.ds(row, 16), :]
            inv = jnp.concatenate([inv] * (PIECE // 128), axis=1)
            for t in range(PIECES):
                here = pl.ds(t * PIECE, PIECE)
                buf[slot, pl.ds(g * 16, 16), here] = (merged[t, pl.ds(row, 16), :] * inv).astype(bf16)
        store(s, slot).start()
        return carry

    lax.fori_loop(0, steps, step, 0)
    for s in range(steps - slots, steps):
        store(s, s % slots).wait()


def normalise(merged, peaks):
    return pl.pallas_call(
        normalise_kernel,
        out_shape=(SDS((DEPTH, WIDTH), bf16), SDS((1, DEPTH), f32)),
        in_specs=[in_vmem(), in_vmem()],
        out_specs=(in_hbm(), in_vmem()),
        scratch_shapes=[
            pltpu.VMEM((DEPTH, 128), f32),
            pltpu.VMEM((4, OUT_ROWS, WIDTH), bf16),
            pltpu.SemaphoreType.DMA((4,)),
        ],
        compiler_params=params_for(16),
        name="normalise",
    )(near(merged), peaks)


def local(codes, scale, pb, pa, mb, vb, ma, va, delta_b, delta_a, tallies):
    exchange = functools.partial(lax.all_to_all, split_axis=0, concat_axis=0, tiled=True)
    mate = functools.partial(lax.ppermute, axis_name="c", perm=[(0, 1), (1, 0)])
    weights = tallies.astype(f32) / (count_scale * 128)
    own_a = delta_a.reshape(RANKS, FULL_A)
    own_b = delta_b.reshape(FULL_B, RANKS).T
    mate_a, mate_b, mate_w = mate(own_a), mate(own_b), mate(weights)
    pb, mb, vb = pb.T, mb.T, vb.T
    block = jnp.concatenate([pb, mb, vb, pb], axis=0)
    other = lax.ppermute(block, "zh", [(0, 1), (1, 0)])
    pairs = pair_sum(weights, mate_w, own_a, mate_a, own_b, mate_b)
    pairs, codes, block, other = lax.optimization_barrier((pairs, codes, block, other))
    got = exchange(pairs.reshape(CHIPS, 16, LANES), ("zl", "y"))
    col_state = x_gather(jnp.concatenate([block, other], axis=0))
    (top,) = decode(codes, 0)
    got, col_state, top = lax.optimization_barrier((got, col_state, top))
    message = row_sum(got)
    codes, message = lax.optimization_barrier((codes, message))
    got = exchange(message, ("c",) + COL)
    low, *state = decode(codes, PART, (pa, ma, va, pb, mb, vb))
    got, low, state = lax.optimization_barrier((got, low, state))
    pa_n, ma_n, va_n, pb_n, mb_n, vb_n, send, factor = server_step(
        got, col_state, state[:3], state[3:]
    )
    ranks = exchange(send, ROW)
    merged, peaks = merge((top, low), scale.reshape(1, DEPTH), spread(factor), ranks)
    out, scales = normalise(merged, exchange(peaks, COL))
    return (out, scales.reshape(DEPTH), pb_n.T, pa_n, mb_n.T, vb_n.T, ma_n, va_n)


def solution(mesh):
    split = Mesh(mesh.devices.reshape(2, 4, 2, 4, 2), ROW + COL)
    tile, everyone = P(ROW, COL), P(ROW + COL, None, None)
    return jax.shard_map(
        local,
        mesh=split,
        in_specs=(tile, P(ROW)) + (tile,) * 6 + (everyone, everyone, P(ROW + COL, None)),
        out_specs=(tile, P(ROW)) + (tile,) * 6,
        check_vma=False,
    )
```

```python
import functools

import jax
import jax.numpy as jnp
from jax import lax
from jax.experimental import pallas as pl
from jax.experimental.pallas import tpu as pltpu
from jax.sharding import Mesh, PartitionSpec as P

first_decay = 0.9
second_decay = 0.99
server_rate = 0.1
adam_floor = 0.001
adapter_scale = 2.0
count_scale = 64.0
fp8_top = 448.0
peak_eps = 1e-06

f32, bf16, i32 = jnp.float32, jnp.bfloat16, jnp.int32
SDS = jax.ShapeDtypeStruct

ROW, COL = ("zl", "y", "c"), ("x", "zh")
CHIPS, COLS = 8, 8
RANKS = 16
DEPTH, WIDTH = 512, 6656
HALF = WIDTH // 2
FULL_B, FULL_A = DEPTH * 16, WIDTH * 8
LANES = HALF + DEPTH
PIECE = 512
PIECES = WIDTH // PIECE


def adaptive_update(param, moment, second, grad):
    moment_next = first_decay * moment + (1.0 - first_decay) * grad
    second_next = second_decay * second + (1.0 - second_decay) * grad * grad
    param_next = param - server_rate * moment_next / (jnp.sqrt(second_next) + adam_floor)
    return (param_next, moment_next, second_next)


def params_for(mib):
    return pltpu.CompilerParams(vmem_limit_bytes=mib << 20)


def in_hbm():
    return pl.BlockSpec(memory_space=pltpu.HBM)


def stay(x):
    return pltpu.with_memory_space_constraint(x, pltpu.HBM)


def near(x):
    return pltpu.with_memory_space_constraint(x, pltpu.VMEM)


def in_any():
    return pl.BlockSpec(memory_space=pl.ANY)


def kept(shape, kind=f32):
    return pltpu.VMEM(shape, kind)


def in_vmem():
    return pl.BlockSpec(memory_space=pltpu.VMEM)


def in_smem():
    return pl.BlockSpec(memory_space=pltpu.SMEM)


DEC_ROWS = 32
SLOTS = 6
TOP = 352


def decode_kernel(first, steps, count, *refs):
    codes, state = refs[0], refs[1 : 1 + count]
    out, held = refs[1 + count], refs[2 + count : 2 + 2 * count]
    buf, done, sems, out_sems, state_sems = refs[2 + 2 * count :]

    def rows(step):
        return pl.ds(pl.multiple_of(step * DEC_ROWS, DEC_ROWS), DEC_ROWS)

    def fetch(step, slot):
        return pltpu.make_async_copy(
            codes.at[rows(step + first // DEC_ROWS), :], buf.at[slot], sems.at[slot]
        )

    def store(step, slot):
        return pltpu.make_async_copy(done.at[slot], out.at[rows(step), :], out_sems.at[slot])

    for s in range(min(SLOTS - 1, steps)):
        fetch(s, s).start()
    moves = [pltpu.make_async_copy(a, b, state_sems.at[q]) for q, (a, b) in enumerate(zip(state, held))]
    for move in moves:
        move.start()

    def step(s, carry):
        slot = lax.rem(s, SLOTS)
        fetch(s, slot).wait()

        @pl.when(s + SLOTS - 1 < steps)
        def _():
            fetch(s + SLOTS - 1, lax.rem(s + SLOTS - 1, SLOTS)).start()

        @pl.when(s >= SLOTS)
        def _():
            store(s - SLOTS, slot).wait()

        def group(g, carry):
            at = pl.ds(pl.multiple_of(g * 16, 16), 16)
            for t in range(PIECES):
                here = pl.ds(t * PIECE, PIECE)
                code = buf[slot, at, here]
                eights = jnp.maximum(jnp.bitwise_and(code, 120), 8)
                value = lax.shift_left(
                    jnp.bitwise_and(code, 127) - eights + 8, lax.shift_right_logical(eights, 3)
                )
                value = jnp.where(code >= 128, -value, value)
                done[slot, at, here] = value.astype(f32).astype(bf16)
            return carry

        lax.fori_loop(0, DEC_ROWS // 16, group, 0)
        store(s, slot).start()
        return carry

    lax.fori_loop(0, steps, step, 0)
    for s in range(max(steps - SLOTS, 0), steps):
        store(s, s % SLOTS).wait()
    for move in moves:
        move.wait()


def decode(codes, first, rows, state=()):
    count = len(state)
    return pl.pallas_call(
        functools.partial(decode_kernel, first, rows // DEC_ROWS, count),
        out_shape=(pltpu.HBM((rows, WIDTH), bf16),) + tuple(kept(x.shape) for x in state),
        in_specs=[in_hbm()] * (1 + count),
        out_specs=(in_hbm(),) + (in_vmem(),) * count,
        scratch_shapes=[
            pltpu.VMEM((SLOTS, DEC_ROWS, WIDTH), i32),
            pltpu.VMEM((SLOTS, DEC_ROWS, WIDTH), bf16),
            pltpu.SemaphoreType.DMA((SLOTS,)),
            pltpu.SemaphoreType.DMA((SLOTS,)),
            pltpu.SemaphoreType.DMA((6,)),
        ],
        compiler_params=params_for(12),
        cost_estimate=pl.CostEstimate(flops=20_000_000, transcendentals=0, bytes_accessed=12_000_000),
        name="decode",
    )(stay(codes), *[stay(x) for x in state])


def own_kernel(a, b, xa, xb, sem_a, sem_b):
    core = lax.axis_index("c")
    moves = [
        pltpu.make_async_copy(b.at[pl.ds(pl.multiple_of(core * 8, 8), 8), :], xb, sem_b)
    ] + [
        pltpu.make_async_copy(
            a.at[:, pl.ds(pl.multiple_of(c * WIDTH + core * HALF, 128), HALF)],
            xa.at[pl.ds(c * 16, 16), :],
            sem_a.at[c],
        )
        for c in range(COLS)
    ]
    for move in moves:
        move.start()
    for move in moves:
        move.wait()


def own_half(a, b):
    return pl.pallas_call(
        own_kernel,
        out_shape=(kept((128, HALF), bf16), kept((8, FULL_B), bf16)),
        in_specs=[in_hbm()] * 2,
        out_specs=(in_vmem(),) * 2,
        scratch_shapes=[pltpu.SemaphoreType.DMA((COLS,)), pltpu.SemaphoreType.DMA],
        compiler_params=params_for(8),
        name="own_half",
    )(stay(a), stay(b))


CHUNKS = (768, 768, 768, 1024)


def pair_kernel(own_w, mate_w, own_a, mate_a, own_b, mate_b, out, buf, sems):
    core = lax.axis_index("c")

    def store(n, start, width):
        here = pl.ds(start, width)
        return pltpu.make_async_copy(buf.at[:, here], out.at[:, here], sems.at[n])

    o = lax.broadcasted_iota(i32, (128, 256), 0)
    k = lax.broadcasted_iota(i32, (128, 256), 1)
    same_block = jnp.bitwise_and(lax.shift_right_logical(o, 1), 7) == jnp.bitwise_and(
        lax.shift_right_logical(k, 4), 7
    )
    rank = lax.shift_right_logical(o, 4) * 2 + jnp.bitwise_and(o, 1)
    same_rank = rank == jnp.bitwise_and(k, 15)
    weight = jnp.where(k < 128, own_w[0, 1], mate_w[0, 1])
    pick = jnp.where(jnp.logical_and(same_block, same_rank), weight, 0.0).astype(bf16)
    start = 0
    for n, width in enumerate(CHUNKS):
        theirs = [
            mate_a[:, pl.ds(pl.multiple_of(c * WIDTH + core * HALF + start, 128), width)]
            for c in range(COLS)
        ]
        both = jnp.concatenate([own_a[:, pl.ds(start, width)]] + theirs, axis=0)
        buf[:, pl.ds(start, width)] = jnp.dot(pick, both, preferred_element_type=f32).astype(bf16)
        store(n, start, width).start()
        start += width
    for j in range(CHIPS):
        halves = []
        for p in range(2):
            at = pl.ds((2 * j + p) * DEPTH, DEPTH)
            theirs = mate_b[pl.ds(pl.multiple_of(core * 8, 8), 8), at]
            halves.append(own_w[0, 0] * own_b[:, at].astype(f32) + mate_w[0, 0] * theirs.astype(f32))
        buf[pl.ds(j * 16, 16), pl.ds(HALF, DEPTH)] = jnp.concatenate(halves, axis=0).astype(bf16)
    store(len(CHUNKS), HALF, DEPTH).start()
    start = 0
    for n, width in enumerate(CHUNKS + (DEPTH,)):
        store(n, start, width).wait()
        start += width


def pair_sum(own_w, mate_w, own_a, mate_a, own_b, mate_b):
    return pl.pallas_call(
        pair_kernel,
        out_shape=pltpu.HBM((CHIPS * 16, LANES), bf16),
        in_specs=[in_smem()] * 2 + [in_vmem()] * 4,
        out_specs=in_hbm(),
        scratch_shapes=[
            pltpu.VMEM((CHIPS * 16, LANES), bf16),
            pltpu.SemaphoreType.DMA((len(CHUNKS) + 1,)),
        ],
        compiler_params=params_for(16),
        name="pair_sum",
    )(own_w, mate_w, *map(near, (own_a, mate_a, own_b, mate_b)))


def row_kernel(got, out, scr):
    total = got[0].astype(f32)
    for j in range(1, CHIPS):
        total = total + got[j].astype(f32)
    scr[:, 0:8, :] = jnp.zeros_like(scr[:, 0:8, :])
    for d in range(16):
        core, col = divmod(d, COLS)
        a = 2 * col + core
        for i in range(7):
            w = min(PIECE, HALF - i * PIECE)
            scr[d, pl.ds(i, 1), pl.ds(0, w)] = total[a : a + 1, i * PIECE : i * PIECE + w]
        scr[d, pl.ds(8, 8), :] = total[core * 8 : core * 8 + 8, HALF:LANES]
    out[...] = scr[...].astype(bf16)


def row_sum(got):
    return pl.pallas_call(
        row_kernel,
        out_shape=SDS((16, 16, PIECE), bf16),
        in_specs=[in_vmem()],
        out_specs=in_vmem(),
        scratch_shapes=[pltpu.VMEM((16, 16, PIECE), f32)],
        compiler_params=params_for(16),
        name="row_sum",
    )(near(got))


def step_kernel(got, pa, ma, va, send, ga, gb, rows):
    for h in range(2):
        acc = jnp.zeros((16, PIECE), f32)
        for c in range(COLS):
            acc = acc + got[h * COLS + c].astype(f32)
        for i in range(7):
            w = min(PIECE, HALF - i * PIECE)
            ga[:, pl.ds(h * HALF + i * PIECE, w)] = acc[i : i + 1, 0:w]
        gb[pl.ds(h * 8, 8), :] = acc[8:16, :]
    pn = adaptive_update(pa[...], ma[...], va[...], ga[...])[0]
    rows[...] = jnp.zeros_like(rows)
    for i in range(PIECES):
        rows[pl.ds(i, 1), :] = pn[:, i * PIECE : (i + 1) * PIECE]
    message = rows[...].astype(bf16)
    for d in range(16):
        send[d] = message


def server_step(got, pa, ma, va):
    return pl.pallas_call(
        step_kernel,
        out_shape=(SDS((16, 16, PIECE), bf16), kept((1, WIDTH)), kept((RANKS, DEPTH))),
        in_specs=[in_vmem()] * 4,
        out_specs=(in_vmem(),) * 3,
        scratch_shapes=[pltpu.VMEM((16, PIECE), f32)],
        compiler_params=params_for(16),
        name="server_step",
    )(*map(near, (got, pa, ma, va)))


APART = (0, 4, 2, 6, 1, 5, 3, 7)


def state_kernel(
    ga, gb, pa, ma, va, pb, mb, vb, col_0, col_1, pa_n, ma_n, va_n, pb_n, mb_n, vb_n, wide, scr
):
    col = lax.axis_index("x") * 2 + lax.axis_index("zh")
    for n, apart in enumerate(APART):
        block = (col_0, col_1)[n // 4][pl.ds(n % 4 * 8, 8), :]
        owner = jnp.bitwise_xor(col, apart)
        for q in range(3):
            scr[q, owner] = block[2 * q : 2 * q + 2, :]
    grad = gb[...]
    whole = [scr[q].reshape(RANKS, DEPTH) for q in range(3)]
    full = adaptive_update(*whole, grad)[0]
    k = lax.broadcasted_iota(i32, (RANKS, 256), 1)
    r = lax.broadcasted_iota(i32, (RANKS, 256), 0)
    repeat = jnp.where(lax.shift_right_logical(k, 4) == r, adapter_scale, 0.0).astype(bf16)
    tall = jnp.transpose(full).astype(bf16)
    wide[...] = jnp.dot(tall, repeat, preferred_element_type=f32).astype(bf16)
    own = [
        jnp.sum(jnp.where(r[:, 0:1] == 2 * col + q, grad, 0.0), axis=0, keepdims=True)
        for q in range(2)
    ]
    pb_n[...], mb_n[...], vb_n[...] = adaptive_update(
        pb[...], mb[...], vb[...], jnp.concatenate(own, axis=0)
    )
    pa_n[...], ma_n[...], va_n[...] = adaptive_update(pa[...], ma[...], va[...], ga[...])


def server_state(ga, gb, a_state, b_state, col_state):
    a_shape, b_shape = SDS((1, WIDTH), f32), SDS((2, DEPTH), f32)
    return pl.pallas_call(
        state_kernel,
        out_shape=(a_shape,) * 3 + (b_shape,) * 3 + (kept((DEPTH, 256), bf16),),
        in_specs=[in_vmem()] * 10,
        out_specs=(in_vmem(),) * 7,
        scratch_shapes=[pltpu.VMEM((3, COLS, 2, DEPTH), f32)],
        compiler_params=params_for(16),
        name="server_state",
    )(*map(near, (ga, gb, *a_state, *b_state)), *col_state)


BLOCK = 512


def merge_kernel(dec_top, dec_low, scale, wide, ranks, merged, peaks, buf, row_scale, tops, sems):
    fetches = []
    for i in range(PIECES):
        here = pl.ds(i * PIECE, PIECE)
        fetches.append(
            [
                pltpu.make_async_copy(dec.at[:, here], buf.at[i, pl.ds(q * TOP, (TOP, DEPTH - TOP)[q]), :], sems.at[i, q])
                for q, dec in enumerate((dec_top, dec_low))
            ]
        )
        for fetch in fetches[-1]:
            fetch.start()
    row_scale[...] = jnp.transpose(jnp.broadcast_to(scale[...] * 2.0**-10, (128, DEPTH)))
    lane = jnp.bitwise_and(lax.broadcasted_iota(i32, (BLOCK, 256), 1), 15)
    right = ranks[...].reshape(256, PIECE)
    tops[...] = jnp.zeros_like(tops)
    for i in range(PIECES):
        for fetch in fetches[i]:
            fetch.wait()
        for b in range(DEPTH // BLOCK):
            at = pl.ds(b * BLOCK, BLOCK)
            left = wide[at, :]
            one = jnp.where(lane == i, left, jnp.zeros_like(left))
            low = jnp.dot(one, right, preferred_element_type=f32)
            top = tops[at, :]
            for t in range(PIECE // 128):
                here = pl.ds(t * 128, 128)
                whole = buf[i, at, here].astype(f32) * row_scale[at, :] + low[:, t * 128 : t * 128 + 128]
                merged[i, at, here] = whole
                top = jnp.maximum(top, jnp.abs(whole))
            tops[at, :] = top
    peak = jnp.max(jnp.transpose(tops[...]), axis=0, keepdims=True)
    for c in range(COLS):
        peaks[c] = peak


def merge(decs, scale, wide, ranks):
    return pl.pallas_call(
        merge_kernel,
        out_shape=(pltpu.VMEM((PIECES, DEPTH, PIECE), f32), SDS((COLS, 1, DEPTH), f32)),
        in_specs=[in_hbm()] * 2 + [in_vmem()] * 3,
        out_specs=(in_vmem(), in_vmem()),
        scratch_shapes=[
            pltpu.VMEM((PIECES, DEPTH, PIECE), bf16),
            pltpu.VMEM((DEPTH, 128), f32),
            pltpu.VMEM((DEPTH, 128), f32),
            pltpu.SemaphoreType.DMA((PIECES, 2)),
        ],
        compiler_params=params_for(16),
        name="merge",
    )(*map(stay, decs), scale, near(wide), near(ranks))


OUT_ROWS = 32


def normalise_kernel(merged, peaks, out, scales, inverse, buf, sems):
    peak = peaks[0]
    for c in range(1, COLS):
        peak = jnp.maximum(peak, peaks[c])
    peak = peak + peak_eps
    scales[...] = peak / fp8_top
    inverse[...] = jnp.transpose(jnp.broadcast_to(1.0 / peak, (128, DEPTH)))
    steps, slots = DEPTH // OUT_ROWS, 8

    def store(step, slot):
        return pltpu.make_async_copy(
            buf.at[slot],
            out.at[pl.ds(pl.multiple_of(step * OUT_ROWS, OUT_ROWS), OUT_ROWS), :],
            sems.at[slot],
        )

    def step(s, carry):
        slot = lax.rem(s, slots)

        @pl.when(s >= slots)
        def _():
            store(s - slots, slot).wait()

        for g in range(OUT_ROWS // 16):
            row = pl.multiple_of(s * OUT_ROWS + g * 16, 16)
            inv = inverse[pl.ds(row, 16), :]
            inv = jnp.concatenate([inv] * (PIECE // 128), axis=1)
            for t in range(PIECES):
                here = pl.ds(t * PIECE, PIECE)
                buf[slot, pl.ds(g * 16, 16), here] = (merged[t, pl.ds(row, 16), :] * inv).astype(bf16)
        store(s, slot).start()
        return carry

    lax.fori_loop(0, steps, step, 0)
    for s in range(steps - slots, steps):
        store(s, s % slots).wait()


def normalise(merged, peaks):
    return pl.pallas_call(
        normalise_kernel,
        out_shape=(SDS((DEPTH, WIDTH), bf16), SDS((1, DEPTH), f32)),
        in_specs=[in_vmem(), in_vmem()],
        out_specs=(in_hbm(), in_vmem()),
        scratch_shapes=[
            pltpu.VMEM((DEPTH, 128), f32),
            pltpu.VMEM((8, OUT_ROWS, WIDTH), bf16),
            pltpu.SemaphoreType.DMA((8,)),
        ],
        compiler_params=params_for(16),
        name="normalise",
    )(near(merged), peaks)


def local(codes, scale, pb, pa, mb, vb, ma, va, delta_b, delta_a, tallies):
    exchange = functools.partial(lax.all_to_all, split_axis=0, concat_axis=0, tiled=True)
    swap = functools.partial(lax.ppermute, perm=[(0, 1), (1, 0)])
    weights = tallies.astype(f32) / (count_scale * 128)
    own_a = delta_a.reshape(RANKS, FULL_A)
    own_b = delta_b.reshape(FULL_B, RANKS).T
    mate_a, mate_b, mate_w = swap(own_a, "c"), swap(own_b, "c"), swap(weights, "c")
    pb, mb, vb = pb.T, mb.T, vb.T
    near_a, near_b = own_half(own_a, own_b)
    pairs = pair_sum(weights, mate_w, near_a, mate_a, near_b, mate_b)
    pairs, codes, pb, mb, vb = lax.optimization_barrier((pairs, codes, pb, mb, vb))
    got = exchange(pairs.reshape(CHIPS, 16, LANES), ("zl", "y"))
    block = jnp.concatenate([pb, mb, vb, pb], axis=0)
    for apart in (2, 1):
        other = lax.ppermute(block, "x", [(k, k ^ apart) for k in range(4)])
        block = jnp.concatenate([block, other], axis=0)
    (top,) = decode(codes, 0, TOP)
    got, top, block = lax.optimization_barrier((got, top, block))
    message = row_sum(got)
    codes, message, block = lax.optimization_barrier((codes, message, block))
    got = exchange(message, ("c",) + COL)
    other = swap(block, "zh")
    low, *state = decode(codes, TOP, DEPTH - TOP, (pa, ma, va, pb, mb, vb))
    got, low, state, other = lax.optimization_barrier((got, low, state, other))
    send, ga, gb = server_step(got, *state[:3])
    ranks = exchange(send, ROW)
    pa_n, ma_n, va_n, pb_n, mb_n, vb_n, wide = server_state(
        ga, gb, state[:3], state[3:], (block, other)
    )
    merged, peaks = merge((top, low), scale.reshape(1, DEPTH), wide, ranks)
    out, scales = normalise(merged, exchange(peaks, COL))
    return (out, scales.reshape(DEPTH), pb_n.T, pa_n, mb_n.T, vb_n.T, ma_n, va_n)


def solution(mesh):
    split = Mesh(mesh.devices.reshape(2, 4, 2, 4, 2), ROW + COL)
    tile, everyone = P(ROW, COL), P(ROW + COL, None, None)
    return jax.shard_map(
        local,
        mesh=split,
        in_specs=(tile, P(ROW)) + (tile,) * 6 + (everyone, everyone, P(ROW + COL, None)),
        out_specs=(tile, P(ROW)) + (tile,) * 6,
        check_vma=False,
    )
```

```python
import functools

import jax
import jax.numpy as jnp
from jax import lax
from jax.experimental import pallas as pl
from jax.experimental.pallas import tpu as pltpu
from jax.sharding import Mesh, PartitionSpec as P

first_decay = 0.9
second_decay = 0.99
server_rate = 0.1
adam_floor = 0.001
adapter_scale = 2.0
count_scale = 64.0
fp8_top = 448.0
peak_eps = 1e-06

f32, bf16, i32 = jnp.float32, jnp.bfloat16, jnp.int32
SDS = jax.ShapeDtypeStruct

ROW, COL = ("zl", "y", "c"), ("x", "zh")
CHIPS, COLS = 8, 8
RANKS = 16
DEPTH, WIDTH = 512, 6656
FULL_B, FULL_A = DEPTH * 16, WIDTH * 8
LANES = WIDTH + 2 * DEPTH
PIECE = 512
PIECES = WIDTH // PIECE


def adaptive_update(param, moment, second, grad):
    moment_next = first_decay * moment + (1.0 - first_decay) * grad
    second_next = second_decay * second + (1.0 - second_decay) * grad * grad
    param_next = param - server_rate * moment_next / (jnp.sqrt(second_next) + adam_floor)
    return (param_next, moment_next, second_next)


def params_for(mib):
    return pltpu.CompilerParams(vmem_limit_bytes=mib << 20)


def in_hbm():
    return pl.BlockSpec(memory_space=pltpu.HBM)


def stay(x):
    return pltpu.with_memory_space_constraint(x, pltpu.HBM)


def near(x):
    return pltpu.with_memory_space_constraint(x, pltpu.VMEM)


def in_any():
    return pl.BlockSpec(memory_space=pl.ANY)


def kept(shape, kind=f32):
    return pltpu.VMEM(shape, kind)


def in_vmem():
    return pl.BlockSpec(memory_space=pltpu.VMEM)


def in_smem():
    return pl.BlockSpec(memory_space=pltpu.SMEM)


DEC_ROWS = 32
SLOTS = 6
ROW_PARTS = (352, 160)


def decode_kernel(first, steps, count, *refs):
    codes, state = refs[0], refs[1 : 1 + count]
    out, held = refs[1 + count], refs[2 + count : 2 + 2 * count]
    buf, done, sems, out_sems, state_sems = refs[2 + 2 * count :]

    def rows(step):
        return pl.ds(pl.multiple_of(step * DEC_ROWS, DEC_ROWS), DEC_ROWS)

    def fetch(step, slot):
        return pltpu.make_async_copy(
            codes.at[rows(step + first // DEC_ROWS), :], buf.at[slot], sems.at[slot]
        )

    def store(step, slot):
        return pltpu.make_async_copy(done.at[slot], out.at[rows(step), :], out_sems.at[slot])

    for s in range(min(SLOTS - 1, steps)):
        fetch(s, s).start()
    pairs = []
    for a, b in zip(state, held):
        if a.shape == b.shape:
            pairs.append((a, b))
        else:
            for i in range(PIECES):
                pairs.append((a.at[:, pl.ds(i * PIECE, PIECE)], b.at[pl.ds(i, 1), :]))
    moves = [pltpu.make_async_copy(a, b, state_sems.at[q]) for q, (a, b) in enumerate(pairs)]
    for move in moves:
        move.start()

    def step(s, carry):
        slot = lax.rem(s, SLOTS)
        fetch(s, slot).wait()

        @pl.when(s + SLOTS - 1 < steps)
        def _():
            fetch(s + SLOTS - 1, lax.rem(s + SLOTS - 1, SLOTS)).start()

        @pl.when(s >= SLOTS)
        def _():
            store(s - SLOTS, slot).wait()

        def group(g, carry):
            at = pl.ds(pl.multiple_of(g * 16, 16), 16)
            for t in range(PIECES):
                here = pl.ds(t * PIECE, PIECE)
                code = buf[slot, at, here]
                eights = jnp.maximum(jnp.bitwise_and(code, 120), 8)
                value = lax.shift_left(
                    jnp.bitwise_and(code, 127) - eights + 8, lax.shift_right_logical(eights, 3)
                )
                value = jnp.where(code >= 128, -value, value)
                done[slot, at, here] = value.astype(f32).astype(bf16)
            return carry

        lax.fori_loop(0, DEC_ROWS // 16, group, 0)
        store(s, slot).start()
        return carry

    lax.fori_loop(0, steps, step, 0)
    for s in range(max(steps - SLOTS, 0), steps):
        store(s, s % SLOTS).wait()
    for move in moves:
        move.wait()


def decode(codes, first, rows, state=()):
    count = len(state)
    return pl.pallas_call(
        functools.partial(decode_kernel, first, rows // DEC_ROWS, count),
        out_shape=(pltpu.HBM((rows, WIDTH), bf16),) + tuple(kept(x.shape if x.shape[0] > 1 else (16, PIECE)) for x in state),
        in_specs=[in_hbm()] * (1 + count),
        out_specs=(in_hbm(),) + (in_vmem(),) * count,
        scratch_shapes=[
            pltpu.VMEM((SLOTS, DEC_ROWS, WIDTH), i32),
            pltpu.VMEM((SLOTS, DEC_ROWS, WIDTH), bf16),
            pltpu.SemaphoreType.DMA((SLOTS,)),
            pltpu.SemaphoreType.DMA((SLOTS,)),
            pltpu.SemaphoreType.DMA((3 * PIECES + 3,)),
        ],
        compiler_params=params_for(12),
        cost_estimate=pl.CostEstimate(flops=20_000_000, transcendentals=0, bytes_accessed=12_000_000),
        name="decode",
    )(stay(codes), *[stay(x) for x in state])


def own_kernel(a, b, xa, xb, sem_a, sem_b):
    moves = [pltpu.make_async_copy(b, xb, sem_b)] + [
        pltpu.make_async_copy(
            a.at[:, pl.ds(c * WIDTH, WIDTH)], xa.at[pl.ds(c * RANKS, RANKS), :], sem_a.at[c]
        )
        for c in range(COLS)
    ]
    for move in moves:
        move.start()
    for move in moves:
        move.wait()


def own_deltas(a, b):
    return pl.pallas_call(
        own_kernel,
        out_shape=(kept((128, WIDTH), bf16), kept((RANKS, FULL_B), bf16)),
        in_specs=[in_hbm()] * 2,
        out_specs=(in_vmem(),) * 2,
        scratch_shapes=[pltpu.SemaphoreType.DMA((COLS,)), pltpu.SemaphoreType.DMA],
        compiler_params=params_for(8),
        name="own_deltas",
    )(stay(a), stay(b))


CHUNKS = (1536, 1536, 1536, 2048)


def pair_kernel(own_w, mate_w, own_a, mate_a, own_b, mate_b, out, buf, sems):
    core = lax.axis_index("c")

    def store(n, start, width):
        here = pl.ds(start, width)
        return pltpu.make_async_copy(buf.at[:, here], out.at[:, here], sems.at[n])

    o = lax.broadcasted_iota(i32, (64, 256), 0)
    k = lax.broadcasted_iota(i32, (64, 256), 1)
    same_block = jnp.bitwise_and(o, 7) == jnp.bitwise_and(lax.shift_right_logical(k, 4), 7)
    same_rank = lax.shift_right_logical(o, 3) * 2 + core == jnp.bitwise_and(k, 15)
    weight = jnp.where(k < 128, own_w[0, 1], mate_w[0, 1])
    pick = jnp.where(jnp.logical_and(same_block, same_rank), weight, 0.0).astype(bf16)
    start = 0
    for n, width in enumerate(CHUNKS):
        theirs = [mate_a[:, pl.ds(c * WIDTH + start, width)] for c in range(COLS)]
        both = jnp.concatenate([own_a[:, pl.ds(start, width)]] + theirs, axis=0)
        buf[:, pl.ds(start, width)] = jnp.dot(pick, both, preferred_element_type=f32).astype(bf16)
        store(n, start, width).start()
        start += width
    for j in range(CHIPS):
        at = pl.ds(pl.multiple_of((2 * j + core) * DEPTH, DEPTH), DEPTH)
        both = own_w[0, 0] * own_b[:, at].astype(f32) + mate_w[0, 0] * mate_b[:, at].astype(f32)
        both = jnp.concatenate([both[0:8, :], both[8:16, :]], axis=1)
        buf[pl.ds(j * 8, 8), pl.ds(WIDTH, 2 * DEPTH)] = both.astype(bf16)
    store(len(CHUNKS), WIDTH, 2 * DEPTH).start()
    start = 0
    for n, width in enumerate(CHUNKS + (2 * DEPTH,)):
        store(n, start, width).wait()
        start += width


def pair_sum(own_w, mate_w, own_a, mate_a, own_b, mate_b):
    return pl.pallas_call(
        pair_kernel,
        out_shape=pltpu.HBM((CHIPS * 8, LANES), bf16),
        in_specs=[in_smem()] * 2 + [in_vmem()] * 4,
        out_specs=in_hbm(),
        scratch_shapes=[
            pltpu.VMEM((CHIPS * 8, LANES), bf16),
            pltpu.SemaphoreType.DMA((len(CHUNKS) + 1,)),
        ],
        compiler_params=params_for(16),
        name="pair_sum",
    )(own_w, mate_w, *map(near, (own_a, mate_a, own_b, mate_b)))


def row_kernel(got, out, scr):
    total = got[0].astype(f32)
    for j in range(1, CHIPS):
        total = total + got[j].astype(f32)
    scr[:, 8:16, :] = jnp.zeros_like(scr[:, 8:16, :])
    for c in range(COLS):
        for i in range(PIECES):
            scr[c, pl.ds(i, 1), :] = total[c : c + 1, i * PIECE : (i + 1) * PIECE]
        scr[c, pl.ds(16, 8), :] = total[:, WIDTH : WIDTH + DEPTH]
        scr[c, pl.ds(24, 8), :] = total[:, WIDTH + DEPTH : LANES]
    out[...] = scr[...].astype(bf16)


def row_sum(got):
    return pl.pallas_call(
        row_kernel,
        out_shape=SDS((COLS, 32, PIECE), bf16),
        in_specs=[in_vmem()],
        out_specs=in_vmem(),
        scratch_shapes=[pltpu.VMEM((COLS, 32, PIECE), f32)],
        compiler_params=params_for(16),
        name="row_sum",
    )(near(got))


def step_kernel(got, pa, ma, va, send, grad):
    total = got[0].astype(f32)
    for c in range(1, COLS):
        total = total + got[c].astype(f32)
    grad[...] = total
    pn = adaptive_update(pa[...], ma[...], va[...], total[0:16, :])[0]
    row = lax.broadcasted_iota(i32, pn.shape, 0)
    message = jnp.where(row < PIECES, pn, 0.0).astype(bf16)
    for d in range(16):
        send[d] = message


def server_step(got, pa, ma, va):
    return pl.pallas_call(
        step_kernel,
        out_shape=(SDS((16, 16, PIECE), bf16), kept((32, PIECE))),
        in_specs=[in_vmem()] * 4,
        out_specs=(in_vmem(),) * 2,
        compiler_params=params_for(16),
        name="server_step",
    )(*map(near, (got, pa, ma, va)))


APART = (0, 1, 4, 5, 2, 3, 6, 7)


def state_kernel(
    sums, pa, ma, va, pb, mb, vb, col_0, col_1, pa_n, ma_n, va_n, pb_n, mb_n, vb_n, wide, scr
):
    col = lax.axis_index("x") * 2 + lax.axis_index("zh")
    for n, apart in enumerate(APART):
        block = (col_0, col_1)[n // 4][pl.ds(n % 4 * 8, 8), :]
        owner = jnp.bitwise_xor(col, apart)
        for q in range(3):
            scr[q, owner] = block[2 * q : 2 * q + 2, :]
    grad = sums[16:32, :]
    whole = [scr[q].reshape(RANKS, DEPTH) for q in range(3)]
    full = adaptive_update(*whole, grad)[0]
    k = lax.broadcasted_iota(i32, (RANKS, 256), 1)
    r = lax.broadcasted_iota(i32, (RANKS, 256), 0)
    repeat = jnp.where(lax.shift_right_logical(k, 4) == r, adapter_scale, 0.0).astype(bf16)
    tall = jnp.transpose(full).astype(bf16)
    wide[...] = jnp.dot(tall, repeat, preferred_element_type=f32).astype(bf16)
    own = [
        jnp.sum(jnp.where(r[:, 0:1] == 2 * col + q, grad, 0.0), axis=0, keepdims=True)
        for q in range(2)
    ]
    pb_n[...], mb_n[...], vb_n[...] = adaptive_update(
        pb[...], mb[...], vb[...], jnp.concatenate(own, axis=0)
    )
    news = adaptive_update(pa[...], ma[...], va[...], sums[0:16, :])
    for ref, new in zip((pa_n, ma_n, va_n), news):
        for i in range(PIECES):
            ref[:, pl.ds(i * PIECE, PIECE)] = new[i : i + 1, :]


def server_state(sums, a_state, b_state, col_state):
    a_shape, b_shape = SDS((1, WIDTH), f32), SDS((2, DEPTH), f32)
    return pl.pallas_call(
        state_kernel,
        out_shape=(a_shape,) * 3 + (b_shape,) * 3 + (kept((DEPTH, 256), bf16),),
        in_specs=[in_vmem()] * 9,
        out_specs=(in_vmem(),) * 7,
        scratch_shapes=[pltpu.VMEM((3, COLS, 2, DEPTH), f32)],
        compiler_params=params_for(16),
        name="server_state",
    )(*map(near, (sums, *a_state, *b_state)), *col_state)


GROUPS = (1, 2, 4, 6)


def merge_kernel(dec_0, dec_1, scale, wide, ranks, merged, peaks, buf, row_scale, tops, sems):
    fetches, piece = [], 0
    for n, count in enumerate(GROUPS):
        here = pl.ds(piece * PIECE, count * PIECE)
        fetches.append([])
        row = 0
        for q, dec in enumerate((dec_0, dec_1)):
            to = buf.at[pl.ds(row, ROW_PARTS[q]), here]
            fetches[-1].append(pltpu.make_async_copy(dec.at[:, here], to, sems.at[n, q]))
            fetches[-1][-1].start()
            row += ROW_PARTS[q]
        piece += count
    row_scale[...] = jnp.transpose(jnp.broadcast_to(scale[...] * 2.0**-10, (128, DEPTH)))
    lane = jnp.bitwise_and(lax.broadcasted_iota(i32, (DEPTH, 256), 1), 15)
    right = ranks[...].reshape(256, PIECE)
    tops[...] = jnp.zeros_like(tops)
    piece = 0
    for n, count in enumerate(GROUPS):
        for fetch in fetches[n]:
            fetch.wait()
        for i in range(piece, piece + count):
            one = jnp.where(lane == i, wide[...], jnp.zeros((DEPTH, 256), bf16))
            low = jnp.dot(one, right, preferred_element_type=f32)
            top = tops[...]
            for t in range(PIECE // 128):
                at = t * 128
                code = buf[:, pl.ds(i * PIECE + at, 128)].astype(f32)
                whole = code * row_scale[...] + low[:, at : at + 128]
                merged[i, :, pl.ds(at, 128)] = whole
                top = jnp.maximum(top, jnp.abs(whole))
            tops[...] = top
        piece += count
    peak = jnp.max(jnp.transpose(tops[...]), axis=0, keepdims=True)
    for c in range(COLS):
        peaks[c] = peak


def merge(decs, scale, wide, ranks):
    return pl.pallas_call(
        merge_kernel,
        out_shape=(pltpu.VMEM((PIECES, DEPTH, PIECE), f32), SDS((COLS, 1, DEPTH), f32)),
        in_specs=[in_hbm()] * 2 + [in_vmem()] * 3,
        out_specs=(in_vmem(), in_vmem()),
        scratch_shapes=[
            pltpu.VMEM((DEPTH, WIDTH), bf16),
            pltpu.VMEM((DEPTH, 128), f32),
            pltpu.VMEM((DEPTH, 128), f32),
            pltpu.SemaphoreType.DMA((len(GROUPS), 2)),
        ],
        compiler_params=params_for(20),
        name="merge",
    )(*map(stay, decs), scale, near(wide), near(ranks))


OUT_ROWS = 32


def normalise_kernel(merged, peaks, out, scales, inverse, buf, sems):
    peak = peaks[0]
    for c in range(1, COLS):
        peak = jnp.maximum(peak, peaks[c])
    peak = peak + peak_eps
    scales[...] = peak / fp8_top
    inverse[...] = jnp.transpose(jnp.broadcast_to(1.0 / peak, (128, DEPTH)))
    steps, slots = DEPTH // OUT_ROWS, 8

    def store(step, slot):
        return pltpu.make_async_copy(
            buf.at[slot],
            out.at[pl.ds(pl.multiple_of(step * OUT_ROWS, OUT_ROWS), OUT_ROWS), :],
            sems.at[slot],
        )

    def step(s, carry):
        slot = lax.rem(s, slots)

        @pl.when(s >= slots)
        def _():
            store(s - slots, slot).wait()

        for g in range(OUT_ROWS // 16):
            row = pl.multiple_of(s * OUT_ROWS + g * 16, 16)
            inv = inverse[pl.ds(row, 16), :]
            inv = jnp.concatenate([inv] * (PIECE // 128), axis=1)
            for t in range(PIECES):
                here = pl.ds(t * PIECE, PIECE)
                buf[slot, pl.ds(g * 16, 16), here] = (merged[t, pl.ds(row, 16), :] * inv).astype(bf16)
        store(s, slot).start()
        return carry

    lax.fori_loop(0, steps, step, 0)
    for s in range(steps - slots, steps):
        store(s, s % slots).wait()


def normalise(merged, peaks):
    return pl.pallas_call(
        normalise_kernel,
        out_shape=(SDS((DEPTH, WIDTH), bf16), SDS((1, DEPTH), f32)),
        in_specs=[in_vmem(), in_vmem()],
        out_specs=(in_hbm(), in_vmem()),
        scratch_shapes=[
            pltpu.VMEM((DEPTH, 128), f32),
            pltpu.VMEM((8, OUT_ROWS, WIDTH), bf16),
            pltpu.SemaphoreType.DMA((8,)),
        ],
        compiler_params=params_for(16),
        name="normalise",
    )(near(merged), peaks)


def local(codes, scale, pb, pa, mb, vb, ma, va, delta_b, delta_a, tallies):
    exchange = functools.partial(lax.all_to_all, split_axis=0, concat_axis=0, tiled=True)
    swap = functools.partial(lax.ppermute, perm=[(0, 1), (1, 0)])
    weights = tallies.astype(f32) / (count_scale * 128)
    own_a = delta_a.reshape(RANKS, FULL_A)
    own_b = delta_b.reshape(FULL_B, RANKS).T
    mate_a, mate_b, mate_w = swap(own_a, "c"), swap(own_b, "c"), swap(weights, "c")
    pb, mb, vb = pb.T, mb.T, vb.T
    block = jnp.concatenate([pb, mb, vb, pb], axis=0)
    other = swap(block, "zh")
    near_a, near_b = own_deltas(own_a, own_b)
    pairs = pair_sum(weights, mate_w, near_a, mate_a, near_b, mate_b)
    pairs, codes, block, other = lax.optimization_barrier((pairs, codes, block, other))
    got = exchange(pairs.reshape(CHIPS, 8, LANES), ("zl", "y"))
    for apart in (2, 1):
        block = jnp.concatenate([block, other], axis=0)
        other = lax.ppermute(block, "x", [(k, k ^ apart) for k in range(4)])
    dec_0, *state = decode(codes, 0, ROW_PARTS[0], (pa, ma, va, pb, mb, vb))
    got, dec_0, block, other, state = lax.optimization_barrier((got, dec_0, block, other, state))
    message = row_sum(got)
    codes, message = lax.optimization_barrier((codes, message))
    got = exchange(message, COL)
    (dec_1,) = decode(codes, *ROW_PARTS)
    got, dec_1 = lax.optimization_barrier((got, dec_1))
    send, sums = server_step(got, *state[:3])
    ranks = exchange(send, ROW)
    pa_n, ma_n, va_n, pb_n, mb_n, vb_n, wide = server_state(
        sums, state[:3], state[3:], (block, other)
    )
    merged, peaks = merge((dec_0, dec_1), scale.reshape(1, DEPTH), wide, ranks)
    out, scales = normalise(merged, exchange(peaks, COL))
    return (out, scales.reshape(DEPTH), pb_n.T, pa_n, mb_n.T, vb_n.T, ma_n, va_n)


def solution(mesh):
    split = Mesh(mesh.devices.reshape(2, 4, 2, 4, 2), ROW + COL)
    tile, everyone = P(ROW, COL), P(ROW + COL, None, None)
    return jax.shard_map(
        local,
        mesh=split,
        in_specs=(tile, P(ROW)) + (tile,) * 6 + (everyone, everyone, P(ROW + COL, None)),
        out_specs=(tile, P(ROW)) + (tile,) * 6,
        check_vma=False,
    )
```

```python
import functools

import jax
import jax.numpy as jnp
from jax import lax
from jax.experimental import pallas as pl
from jax.experimental.pallas import tpu as pltpu
from jax.sharding import Mesh, PartitionSpec as P

first_decay = 0.9
second_decay = 0.99
server_rate = 0.1
adam_floor = 0.001
adapter_scale = 2.0
count_scale = 64.0
fp8_top = 448.0
peak_eps = 1e-06

f32, bf16, i32 = jnp.float32, jnp.bfloat16, jnp.int32
SDS = jax.ShapeDtypeStruct

ROW, COL = ("zl", "y", "c"), ("x", "zh")
CLIENTS = 128
CHIPS, COLS = 8, 8
RANKS = 16
DEPTH, WIDTH = 512, 6656
FULL_B, FULL_A = DEPTH * 16, WIDTH * 8
LANES = WIDTH + 2 * DEPTH
PIECE = 512
PIECES = WIDTH // PIECE


def adaptive_update(param, moment, second, grad):
    moment_next = first_decay * moment + (1.0 - first_decay) * grad
    second_next = second_decay * second + (1.0 - second_decay) * grad * grad
    param_next = param - server_rate * moment_next / (jnp.sqrt(second_next) + adam_floor)
    return (param_next, moment_next, second_next)


def params_for(mib):
    return pltpu.CompilerParams(vmem_limit_bytes=mib << 20)


def in_hbm():
    return pl.BlockSpec(memory_space=pltpu.HBM)


def stay(x):
    return pltpu.with_memory_space_constraint(x, pltpu.HBM)


def near(x):
    return pltpu.with_memory_space_constraint(x, pltpu.VMEM)


def in_any():
    return pl.BlockSpec(memory_space=pl.ANY)


def kept(shape, kind=f32):
    return pltpu.VMEM(shape, kind)


def in_vmem():
    return pl.BlockSpec(memory_space=pltpu.VMEM)


DEC_ROWS = 32
SLOTS = 6
ROW_PARTS = (320, 192)


def decode_kernel(first, steps, count, *refs):
    codes, state = refs[0], refs[1 : 1 + count]
    out, held = refs[1 + count], refs[2 + count : 2 + 2 * count]
    buf, done, sems, out_sems, state_sems = refs[2 + 2 * count :]

    def rows(step):
        return pl.ds(pl.multiple_of(step * DEC_ROWS, DEC_ROWS), DEC_ROWS)

    def fetch(step, slot):
        return pltpu.make_async_copy(
            codes.at[rows(step + first // DEC_ROWS), :], buf.at[slot], sems.at[slot]
        )

    def store(step, slot):
        return pltpu.make_async_copy(done.at[slot], out.at[rows(step), :], out_sems.at[slot])

    for s in range(min(SLOTS - 1, steps)):
        fetch(s, s).start()
    pairs = []
    for a, b in zip(state, held):
        if a.shape == b.shape:
            pairs.append((a, b))
        else:
            for i in range(PIECES):
                pairs.append((a.at[:, pl.ds(i * PIECE, PIECE)], b.at[pl.ds(i, 1), :]))
    moves = [pltpu.make_async_copy(a, b, state_sems.at[q]) for q, (a, b) in enumerate(pairs)]
    for move in moves:
        move.start()

    def step(s, carry):
        slot = lax.rem(s, SLOTS)
        fetch(s, slot).wait()

        @pl.when(s + SLOTS - 1 < steps)
        def _():
            fetch(s + SLOTS - 1, lax.rem(s + SLOTS - 1, SLOTS)).start()

        @pl.when(s >= SLOTS)
        def _():
            store(s - SLOTS, slot).wait()

        def group(g, carry):
            at = pl.ds(pl.multiple_of(g * 16, 16), 16)
            for t in range(PIECES):
                here = pl.ds(t * PIECE, PIECE)
                code = buf[slot, at, here]
                eights = jnp.maximum(jnp.bitwise_and(code, 120), 8)
                value = lax.shift_left(
                    jnp.bitwise_and(code, 127) - eights + 8, lax.shift_right_logical(eights, 3)
                )
                value = jnp.where(code >= 128, -value, value)
                done[slot, at, here] = value.astype(f32).astype(bf16)
            return carry

        lax.fori_loop(0, DEC_ROWS // 16, group, 0)
        store(s, slot).start()
        return carry

    lax.fori_loop(0, steps, step, 0)
    for s in range(max(steps - SLOTS, 0), steps):
        store(s, s % SLOTS).wait()
    for move in moves:
        move.wait()


def decode(codes, first, rows, state=()):
    count = len(state)
    return pl.pallas_call(
        functools.partial(decode_kernel, first, rows // DEC_ROWS, count),
        out_shape=(pltpu.HBM((rows, WIDTH), bf16),) + tuple(kept(x.shape if x.shape[0] > 1 else (16, PIECE)) for x in state),
        in_specs=[in_hbm()] * (1 + count),
        out_specs=(in_hbm(),) + (in_vmem(),) * count,
        scratch_shapes=[
            pltpu.VMEM((SLOTS, DEC_ROWS, WIDTH), i32),
            pltpu.VMEM((SLOTS, DEC_ROWS, WIDTH), bf16),
            pltpu.SemaphoreType.DMA((SLOTS,)),
            pltpu.SemaphoreType.DMA((SLOTS,)),
            pltpu.SemaphoreType.DMA((3 * PIECES + 3,)),
        ],
        compiler_params=params_for(12),
        cost_estimate=pl.CostEstimate(flops=20_000_000, transcendentals=0, bytes_accessed=12_000_000),
        name="decode",
    )(stay(codes), *[stay(x) for x in state])


def own_kernel(n, a, b, xn, xa, xb, sem_a, sem_b, sem_n):
    moves = [pltpu.make_async_copy(b, xb, sem_b), pltpu.make_async_copy(n, xn, sem_n)] + [
        pltpu.make_async_copy(
            a.at[:, pl.ds(c * WIDTH, WIDTH)], xa.at[pl.ds(c * RANKS, RANKS), :], sem_a.at[c]
        )
        for c in range(COLS)
    ]
    for move in moves:
        move.start()
    for move in moves:
        move.wait()


def own_deltas(n, a, b):
    return pl.pallas_call(
        own_kernel,
        out_shape=(kept((1, 2), i32), kept((128, WIDTH), bf16), kept((RANKS, FULL_B), bf16)),
        in_specs=[in_hbm()] * 3,
        out_specs=(in_vmem(),) * 3,
        scratch_shapes=[pltpu.SemaphoreType.DMA((COLS,))] + [pltpu.SemaphoreType.DMA] * 2,
        compiler_params=params_for(8),
        name="own_deltas",
    )(stay(n), stay(a), stay(b))


CHUNKS = (1536, 1536, 1536, 2048)


def pair_kernel(own_n, mate_n, own_a, mate_a, own_b, mate_b, out, buf, sems):
    core = lax.axis_index("c")

    def store(n, start, width):
        here = pl.ds(start, width)
        return pltpu.make_async_copy(buf.at[:, here], out.at[:, here], sems.at[n])

    weights = [n[...].astype(f32) / (count_scale * CLIENTS) for n in (own_n, mate_n)]
    own_w, mate_w = ((w[:, 0:1], w[:, 1:2]) for w in weights)
    o = lax.broadcasted_iota(i32, (64, 256), 0)
    k = lax.broadcasted_iota(i32, (64, 256), 1)
    same_block = jnp.bitwise_and(o, 7) == jnp.bitwise_and(lax.shift_right_logical(k, 4), 7)
    same_rank = lax.shift_right_logical(o, 3) * 2 + core == jnp.bitwise_and(k, 15)
    weight = jnp.where(k < 128, own_w[1], mate_w[1])
    pick = jnp.where(jnp.logical_and(same_block, same_rank), weight, 0.0).astype(bf16)
    start = 0
    for n, width in enumerate(CHUNKS):
        theirs = [mate_a[:, pl.ds(c * WIDTH + start, width)] for c in range(COLS)]
        both = jnp.concatenate([own_a[:, pl.ds(start, width)]] + theirs, axis=0)
        buf[:, pl.ds(start, width)] = jnp.dot(pick, both, preferred_element_type=f32).astype(bf16)
        store(n, start, width).start()
        start += width
    for j in range(CHIPS):
        at = pl.ds(pl.multiple_of((2 * j + core) * DEPTH, DEPTH), DEPTH)
        both = own_w[0] * own_b[:, at].astype(f32) + mate_w[0] * mate_b[:, at].astype(f32)
        both = jnp.concatenate([both[0:8, :], both[8:16, :]], axis=1)
        buf[pl.ds(j * 8, 8), pl.ds(WIDTH, 2 * DEPTH)] = both.astype(bf16)
    store(len(CHUNKS), WIDTH, 2 * DEPTH).start()
    start = 0
    for n, width in enumerate(CHUNKS + (2 * DEPTH,)):
        store(n, start, width).wait()
        start += width


def pair_sum(own_n, mate_n, own_a, mate_a, own_b, mate_b):
    return pl.pallas_call(
        pair_kernel,
        out_shape=pltpu.HBM((CHIPS * 8, LANES), bf16),
        in_specs=[in_vmem()] * 6,
        out_specs=in_hbm(),
        scratch_shapes=[
            pltpu.VMEM((CHIPS * 8, LANES), bf16),
            pltpu.SemaphoreType.DMA((len(CHUNKS) + 1,)),
        ],
        compiler_params=params_for(16),
        name="pair_sum",
    )(*map(near, (own_n, mate_n, own_a, mate_a, own_b, mate_b)))


def row_kernel(got, out, scr):
    total = got[0].astype(f32)
    for j in range(1, CHIPS):
        total = total + got[j].astype(f32)
    scr[:, 8:16, :] = jnp.zeros_like(scr[:, 8:16, :])
    for c in range(COLS):
        for i in range(PIECES):
            scr[c, pl.ds(i, 1), :] = total[c : c + 1, i * PIECE : (i + 1) * PIECE]
        scr[c, pl.ds(16, 8), :] = total[:, WIDTH : WIDTH + DEPTH]
        scr[c, pl.ds(24, 8), :] = total[:, WIDTH + DEPTH : LANES]
    out[...] = scr[...].astype(bf16)


def row_sum(got):
    return pl.pallas_call(
        row_kernel,
        out_shape=SDS((COLS, 32, PIECE), bf16),
        in_specs=[in_vmem()],
        out_specs=in_vmem(),
        scratch_shapes=[pltpu.VMEM((COLS, 32, PIECE), f32)],
        compiler_params=params_for(16),
        name="row_sum",
    )(near(got))


def step_kernel(got, pa, ma, va, send, grad):
    total = got[0].astype(f32)
    for c in range(1, COLS):
        total = total + got[c].astype(f32)
    grad[...] = total
    pn = adaptive_update(pa[...], ma[...], va[...], total[0:16, :])[0]
    row = lax.broadcasted_iota(i32, pn.shape, 0)
    message = jnp.where(row < PIECES, pn, 0.0).astype(bf16)
    for d in range(CHIPS):
        send[d] = message


def server_step(got, pa, ma, va):
    return pl.pallas_call(
        step_kernel,
        out_shape=(SDS((CHIPS, 16, PIECE), bf16), kept((32, PIECE))),
        in_specs=[in_vmem()] * 4,
        out_specs=(in_vmem(),) * 2,
        compiler_params=params_for(16),
        name="server_step",
    )(*map(near, (got, pa, ma, va)))


APART = (0, 1, 4, 5, 2, 3, 6, 7)


def state_kernel(
    sums, pa, ma, va, pb, mb, vb, col_0, col_1, pa_n, ma_n, va_n, pb_n, mb_n, vb_n, wide, scr
):
    col = lax.axis_index("x") * 2 + lax.axis_index("zh")
    for n, apart in enumerate(APART):
        block = (col_0, col_1)[n // 4][pl.ds(n % 4 * 8, 8), :]
        owner = jnp.bitwise_xor(col, apart)
        for q in range(3):
            scr[q, owner] = block[2 * q : 2 * q + 2, :]
    grad = sums[16:32, :]
    whole = [scr[q].reshape(RANKS, DEPTH) for q in range(3)]
    full = adaptive_update(*whole, grad)[0]
    k = lax.broadcasted_iota(i32, (RANKS, 256), 1)
    r = lax.broadcasted_iota(i32, (RANKS, 256), 0)
    core = lax.axis_index("c")
    parity = jnp.bitwise_xor(lax.shift_right_logical(k, 7), core)
    rank = jnp.bitwise_and(lax.shift_right_logical(k, 4), 7) * 2 + parity
    repeat = jnp.where(rank == r, adapter_scale, 0.0).astype(bf16)
    tall = jnp.transpose(full).astype(bf16)
    wide[...] = jnp.dot(tall, repeat, preferred_element_type=f32).astype(bf16)
    own = [
        jnp.sum(jnp.where(r[:, 0:1] == 2 * col + q, grad, 0.0), axis=0, keepdims=True)
        for q in range(2)
    ]
    pb_n[...], mb_n[...], vb_n[...] = adaptive_update(
        pb[...], mb[...], vb[...], jnp.concatenate(own, axis=0)
    )
    news = adaptive_update(pa[...], ma[...], va[...], sums[0:16, :])
    for ref, new in zip((pa_n, ma_n, va_n), news):
        for i in range(PIECES):
            ref[:, pl.ds(i * PIECE, PIECE)] = new[i : i + 1, :]


def server_state(sums, a_state, b_state, col_state):
    a_shape, b_shape = SDS((1, WIDTH), f32), SDS((2, DEPTH), f32)
    return pl.pallas_call(
        state_kernel,
        out_shape=(a_shape,) * 3 + (b_shape,) * 3 + (kept((DEPTH, 256), bf16),),
        in_specs=[in_vmem()] * 9,
        out_specs=(in_vmem(),) * 7,
        scratch_shapes=[pltpu.VMEM((3, COLS, 2, DEPTH), f32)],
        compiler_params=params_for(16),
        name="server_state",
    )(*map(near, (sums, *a_state, *b_state)), *col_state)


GROUPS = (1, 2, 4, 6)


def merge_kernel(dec_0, dec_1, scale, wide, ranks, mate_ranks, merged, peaks, buf, row_scale, tops, sems):
    fetches, piece = [], 0
    for n, count in enumerate(GROUPS):
        here = pl.ds(piece * PIECE, count * PIECE)
        fetches.append([])
        row = 0
        for q, dec in enumerate((dec_0, dec_1)):
            to = buf.at[pl.ds(row, ROW_PARTS[q]), here]
            fetches[-1].append(pltpu.make_async_copy(dec.at[:, here], to, sems.at[n, q]))
            fetches[-1][-1].start()
            row += ROW_PARTS[q]
        piece += count
    row_scale[...] = jnp.transpose(jnp.broadcast_to(scale[...] * 2.0**-10, (128, DEPTH)))
    lane = jnp.bitwise_and(lax.broadcasted_iota(i32, (DEPTH, 256), 1), 15)
    right = jnp.concatenate([r[...].reshape(128, PIECE) for r in (ranks, mate_ranks)], axis=0)
    tops[...] = jnp.zeros_like(tops)
    piece = 0
    for n, count in enumerate(GROUPS):
        for fetch in fetches[n]:
            fetch.wait()
        for i in range(piece, piece + count):
            one = jnp.where(lane == i, wide[...], jnp.zeros((DEPTH, 256), bf16))
            low = jnp.dot(one, right, preferred_element_type=f32)
            top = tops[...]
            for t in range(PIECE // 128):
                at = t * 128
                code = buf[:, pl.ds(i * PIECE + at, 128)].astype(f32)
                whole = code * row_scale[...] + low[:, at : at + 128]
                merged[i, :, pl.ds(at, 128)] = whole
                top = jnp.maximum(top, jnp.abs(whole))
            tops[...] = top
        piece += count
    peak = jnp.max(jnp.transpose(tops[...]), axis=0, keepdims=True)
    for c in range(COLS):
        peaks[c] = peak


def merge(decs, scale, wide, ranks, mate_ranks):
    return pl.pallas_call(
        merge_kernel,
        out_shape=(pltpu.VMEM((PIECES, DEPTH, PIECE), f32), SDS((COLS, 1, DEPTH), f32)),
        in_specs=[in_hbm()] * 2 + [in_vmem()] * 4,
        out_specs=(in_vmem(), in_vmem()),
        scratch_shapes=[
            pltpu.VMEM((DEPTH, WIDTH), bf16),
            pltpu.VMEM((DEPTH, 128), f32),
            pltpu.VMEM((DEPTH, 128), f32),
            pltpu.SemaphoreType.DMA((len(GROUPS), 2)),
        ],
        compiler_params=params_for(20),
        name="merge",
    )(*map(stay, decs), scale, near(wide), near(ranks), near(mate_ranks))


OUT_ROWS = 32


def normalise_kernel(merged, peaks, out, scales, inverse, buf, sems):
    peak = peaks[0]
    for c in range(1, COLS):
        peak = jnp.maximum(peak, peaks[c])
    peak = peak + peak_eps
    scales[...] = peak / fp8_top
    inverse[...] = jnp.transpose(jnp.broadcast_to(1.0 / peak, (128, DEPTH)))
    steps, slots = DEPTH // OUT_ROWS, 8

    def store(step, slot):
        return pltpu.make_async_copy(
            buf.at[slot],
            out.at[pl.ds(pl.multiple_of(step * OUT_ROWS, OUT_ROWS), OUT_ROWS), :],
            sems.at[slot],
        )

    def step(s, carry):
        slot = lax.rem(s, slots)

        @pl.when(s >= slots)
        def _():
            store(s - slots, slot).wait()

        for g in range(OUT_ROWS // 16):
            row = pl.multiple_of(s * OUT_ROWS + g * 16, 16)
            inv = inverse[pl.ds(row, 16), :]
            inv = jnp.concatenate([inv] * (PIECE // 128), axis=1)
            for t in range(PIECES):
                here = pl.ds(t * PIECE, PIECE)
                buf[slot, pl.ds(g * 16, 16), here] = (merged[t, pl.ds(row, 16), :] * inv).astype(bf16)
        store(s, slot).start()
        return carry

    lax.fori_loop(0, steps, step, 0)
    for s in range(steps - slots, steps):
        store(s, s % slots).wait()


def normalise(merged, peaks):
    return pl.pallas_call(
        normalise_kernel,
        out_shape=(SDS((DEPTH, WIDTH), bf16), SDS((1, DEPTH), f32)),
        in_specs=[in_vmem(), in_vmem()],
        out_specs=(in_hbm(), in_vmem()),
        scratch_shapes=[
            pltpu.VMEM((DEPTH, 128), f32),
            pltpu.VMEM((8, OUT_ROWS, WIDTH), bf16),
            pltpu.SemaphoreType.DMA((8,)),
        ],
        compiler_params=params_for(16),
        name="normalise",
    )(near(merged), peaks)


def local(codes, scale, pb, pa, mb, vb, ma, va, delta_b, delta_a, tallies):
    exchange = functools.partial(lax.all_to_all, split_axis=0, concat_axis=0, tiled=True)
    swap = functools.partial(lax.ppermute, perm=[(0, 1), (1, 0)])
    own_a = delta_a.reshape(RANKS, FULL_A)
    own_b = delta_b.reshape(FULL_B, RANKS).T
    mate_a, mate_b, mate_n = swap(own_a, "c"), swap(own_b, "c"), swap(tallies, "c")
    pb, mb, vb = pb.T, mb.T, vb.T
    block = jnp.concatenate([pb, mb, vb, pb], axis=0)
    other = swap(block, "zh")
    own_n, own_a, own_b = own_deltas(tallies, own_a, own_b)
    pairs = pair_sum(own_n, mate_n, own_a, mate_a, own_b, mate_b)
    pairs, codes, block, other = lax.optimization_barrier((pairs, codes, block, other))
    got = exchange(pairs.reshape(CHIPS, 8, LANES), ("zl", "y"))
    for apart in (2, 1):
        block = jnp.concatenate([block, other], axis=0)
        other = lax.ppermute(block, "x", [(k, k ^ apart) for k in range(4)])
    dec_0, *state = decode(codes, 0, ROW_PARTS[0], (pa, ma, va, pb, mb, vb))
    got, dec_0, block, other, state = lax.optimization_barrier((got, dec_0, block, other, state))
    message = row_sum(got)
    codes, message = lax.optimization_barrier((codes, message))
    got = exchange(message, COL)
    (dec_1,) = decode(codes, *ROW_PARTS)
    got, dec_1 = lax.optimization_barrier((got, dec_1))
    send, sums = server_step(got, *state[:3])
    ranks = exchange(send, ("zl", "y"))
    pa_n, ma_n, va_n, pb_n, mb_n, vb_n, wide = server_state(
        sums, state[:3], state[3:], (block, other)
    )
    merged, peaks = merge((dec_0, dec_1), scale.reshape(1, DEPTH), wide, ranks, swap(ranks, "c"))
    out, scales = normalise(merged, exchange(peaks, COL))
    return (out, scales.reshape(DEPTH), pb_n.T, pa_n, mb_n.T, vb_n.T, ma_n, va_n)


def solution(mesh):
    split = Mesh(mesh.devices.reshape(2, 4, 2, 4, 2), ROW + COL)
    tile, everyone = P(ROW, COL), P(ROW + COL, None, None)
    return jax.shard_map(
        local,
        mesh=split,
        in_specs=(tile, P(ROW)) + (tile,) * 6 + (everyone, everyone, P(ROW + COL, None)),
        out_specs=(tile, P(ROW)) + (tile,) * 6,
        check_vma=False,
    )
```

```python
import functools

import jax
import jax.numpy as jnp
from jax import lax
from jax.experimental import pallas as pl
from jax.experimental.pallas import tpu as pltpu
from jax.sharding import Mesh, PartitionSpec as P

first_decay = 0.9
second_decay = 0.99
server_rate = 0.1
adam_floor = 0.001
adapter_scale = 2.0
count_scale = 64.0
fp8_top = 448.0
peak_eps = 1e-06

f32, bf16, i32 = jnp.float32, jnp.bfloat16, jnp.int32
f8 = jnp.float8_e4m3fn
SDS = jax.ShapeDtypeStruct

ROW, COL = ("zl", "y", "c"), ("x", "zh")
CLIENTS = 128
CHIPS, COLS = 8, 8
RANKS = 16
DEPTH, WIDTH = 512, 6656
FULL_B, FULL_A = DEPTH * 16, WIDTH * 8
LANES = WIDTH + 2 * DEPTH
PIECE = 512
PIECES = WIDTH // PIECE


def adaptive_update(param, moment, second, grad):
    moment_next = first_decay * moment + (1.0 - first_decay) * grad
    second_next = second_decay * second + (1.0 - second_decay) * grad * grad
    param_next = param - server_rate * moment_next / (jnp.sqrt(second_next) + adam_floor)
    return (param_next, moment_next, second_next)


def params_for(mib):
    return pltpu.CompilerParams(vmem_limit_bytes=mib << 20)


def in_hbm():
    return pl.BlockSpec(memory_space=pltpu.HBM)


def stay(x):
    return pltpu.with_memory_space_constraint(x, pltpu.HBM)


def near(x):
    return pltpu.with_memory_space_constraint(x, pltpu.VMEM)


def in_any():
    return pl.BlockSpec(memory_space=pl.ANY)


def kept(shape, kind=f32):
    return pltpu.VMEM(shape, kind)


def in_vmem():
    return pl.BlockSpec(memory_space=pltpu.VMEM)


DEC_ROWS = 32
SLOTS = 6
ROW_PARTS = (320, 192)


def decode_kernel(first, steps, count, *refs):
    codes, state = refs[0], refs[1 : 1 + count]
    out, held = refs[1 + count], refs[2 + count : 2 + 2 * count]
    buf, done, sems, out_sems, state_sems = refs[2 + 2 * count :]

    def rows(step):
        return pl.ds(pl.multiple_of(step * DEC_ROWS, DEC_ROWS), DEC_ROWS)

    def fetch(step, slot):
        return pltpu.make_async_copy(
            codes.at[rows(step + first // DEC_ROWS), :], buf.at[slot], sems.at[slot]
        )

    def store(step, slot):
        return pltpu.make_async_copy(done.at[slot], out.at[rows(step), :], out_sems.at[slot])

    for s in range(min(SLOTS - 1, steps)):
        fetch(s, s).start()
    pairs = []
    for a, b in zip(state, held):
        if a.shape == b.shape:
            pairs.append((a, b))
        else:
            for i in range(PIECES):
                pairs.append((a.at[:, pl.ds(i * PIECE, PIECE)], b.at[pl.ds(i, 1), :]))
    moves = [pltpu.make_async_copy(a, b, state_sems.at[q]) for q, (a, b) in enumerate(pairs)]
    for move in moves:
        move.start()

    def step(s, carry):
        slot = lax.rem(s, SLOTS)
        fetch(s, slot).wait()

        @pl.when(s + SLOTS - 1 < steps)
        def _():
            fetch(s + SLOTS - 1, lax.rem(s + SLOTS - 1, SLOTS)).start()

        @pl.when(s >= SLOTS)
        def _():
            store(s - SLOTS, slot).wait()

        def group(g, carry):
            at = pl.ds(pl.multiple_of(g * 32, 32), 32)
            for t in range(PIECES):
                here = pl.ds(t * PIECE, PIECE)
                code = buf[slot, at, here]
                eights = jnp.maximum(jnp.bitwise_and(code, 120), 8)
                value = lax.shift_left(
                    jnp.bitwise_and(code, 127) - eights + 8, lax.shift_right_logical(eights, 3)
                )
                value = jnp.where(code >= 128, -value, value)
                done[slot, at, here] = (value.astype(f32) * 2.0**-10).astype(f8)
            return carry

        lax.fori_loop(0, DEC_ROWS // 32, group, 0)
        store(s, slot).start()
        return carry

    lax.fori_loop(0, steps, step, 0)
    for s in range(max(steps - SLOTS, 0), steps):
        store(s, s % SLOTS).wait()
    for move in moves:
        move.wait()


def decode(codes, first, rows, state=()):
    count = len(state)
    return pl.pallas_call(
        functools.partial(decode_kernel, first, rows // DEC_ROWS, count),
        out_shape=(pltpu.HBM((rows, WIDTH), f8),) + tuple(kept(x.shape if x.shape[0] > 1 else (16, PIECE)) for x in state),
        in_specs=[in_hbm()] * (1 + count),
        out_specs=(in_hbm(),) + (in_vmem(),) * count,
        scratch_shapes=[
            pltpu.VMEM((SLOTS, DEC_ROWS, WIDTH), i32),
            pltpu.VMEM((SLOTS, DEC_ROWS, WIDTH), f8),
            pltpu.SemaphoreType.DMA((SLOTS,)),
            pltpu.SemaphoreType.DMA((SLOTS,)),
            pltpu.SemaphoreType.DMA((3 * PIECES + 3,)),
        ],
        compiler_params=params_for(12),
        cost_estimate=pl.CostEstimate(flops=20_000_000, transcendentals=0, bytes_accessed=12_000_000),
        name="decode",
    )(stay(codes), *[stay(x) for x in state])


def own_kernel(n, a, b, xn, xa, xb, sem_a, sem_b, sem_n):
    moves = [pltpu.make_async_copy(b, xb, sem_b), pltpu.make_async_copy(n, xn, sem_n)] + [
        pltpu.make_async_copy(
            a.at[:, pl.ds(c * WIDTH, WIDTH)], xa.at[pl.ds(c * RANKS, RANKS), :], sem_a.at[c]
        )
        for c in range(COLS)
    ]
    for move in moves:
        move.start()
    for move in moves:
        move.wait()


def own_deltas(n, a, b):
    return pl.pallas_call(
        own_kernel,
        out_shape=(kept((1, 2), i32), kept((128, WIDTH), bf16), kept((RANKS, FULL_B), bf16)),
        in_specs=[in_hbm()] * 3,
        out_specs=(in_vmem(),) * 3,
        scratch_shapes=[pltpu.SemaphoreType.DMA((COLS,))] + [pltpu.SemaphoreType.DMA] * 2,
        compiler_params=params_for(8),
        name="own_deltas",
    )(stay(n), stay(a), stay(b))


CHUNKS = (1536, 1536, 1536, 2048)


def pair_kernel(own_n, mate_n, own_a, mate_a, own_b, mate_b, out, buf, sems):
    core = lax.axis_index("c")

    def store(n, start, width):
        here = pl.ds(start, width)
        return pltpu.make_async_copy(buf.at[:, here], out.at[:, here], sems.at[n])

    weights = [n[...].astype(f32) / (count_scale * CLIENTS) for n in (own_n, mate_n)]
    own_w, mate_w = ((w[:, 0:1], w[:, 1:2]) for w in weights)
    o = lax.broadcasted_iota(i32, (64, 256), 0)
    k = lax.broadcasted_iota(i32, (64, 256), 1)
    same_block = jnp.bitwise_and(o, 7) == jnp.bitwise_and(lax.shift_right_logical(k, 4), 7)
    same_rank = lax.shift_right_logical(o, 3) * 2 + core == jnp.bitwise_and(k, 15)
    weight = jnp.where(k < 128, own_w[1], mate_w[1])
    pick = jnp.where(jnp.logical_and(same_block, same_rank), weight, 0.0).astype(bf16)
    start = 0
    for n, width in enumerate(CHUNKS):
        theirs = [mate_a[:, pl.ds(c * WIDTH + start, width)] for c in range(COLS)]
        both = jnp.concatenate([own_a[:, pl.ds(start, width)]] + theirs, axis=0)
        buf[:, pl.ds(start, width)] = jnp.dot(pick, both, preferred_element_type=f32).astype(bf16)
        store(n, start, width).start()
        start += width
    for j in range(CHIPS):
        at = pl.ds(pl.multiple_of((2 * j + core) * DEPTH, DEPTH), DEPTH)
        both = own_w[0] * own_b[:, at].astype(f32) + mate_w[0] * mate_b[:, at].astype(f32)
        both = jnp.concatenate([both[0:8, :], both[8:16, :]], axis=1)
        buf[pl.ds(j * 8, 8), pl.ds(WIDTH, 2 * DEPTH)] = both.astype(bf16)
    store(len(CHUNKS), WIDTH, 2 * DEPTH).start()
    start = 0
    for n, width in enumerate(CHUNKS + (2 * DEPTH,)):
        store(n, start, width).wait()
        start += width


def pair_sum(own_n, mate_n, own_a, mate_a, own_b, mate_b):
    return pl.pallas_call(
        pair_kernel,
        out_shape=pltpu.HBM((CHIPS * 8, LANES), bf16),
        in_specs=[in_vmem()] * 6,
        out_specs=in_hbm(),
        scratch_shapes=[
            pltpu.VMEM((CHIPS * 8, LANES), bf16),
            pltpu.SemaphoreType.DMA((len(CHUNKS) + 1,)),
        ],
        compiler_params=params_for(16),
        name="pair_sum",
    )(*map(near, (own_n, mate_n, own_a, mate_a, own_b, mate_b)))


def row_kernel(got, out, scr):
    total = got[0].astype(f32)
    for j in range(1, CHIPS):
        total = total + got[j].astype(f32)
    scr[:, 8:16, :] = jnp.zeros_like(scr[:, 8:16, :])
    for c in range(COLS):
        for i in range(PIECES):
            scr[c, pl.ds(i, 1), :] = total[c : c + 1, i * PIECE : (i + 1) * PIECE]
        scr[c, pl.ds(16, 8), :] = total[:, WIDTH : WIDTH + DEPTH]
        scr[c, pl.ds(24, 8), :] = total[:, WIDTH + DEPTH : LANES]
    out[...] = scr[...].astype(bf16)


def row_sum(got):
    return pl.pallas_call(
        row_kernel,
        out_shape=SDS((COLS, 32, PIECE), bf16),
        in_specs=[in_vmem()],
        out_specs=in_vmem(),
        scratch_shapes=[pltpu.VMEM((COLS, 32, PIECE), f32)],
        compiler_params=params_for(16),
        name="row_sum",
    )(near(got))


def step_kernel(got, pa, ma, va, send, grad):
    total = got[0].astype(f32)
    for c in range(1, COLS):
        total = total + got[c].astype(f32)
    grad[...] = total
    pn = adaptive_update(pa[...], ma[...], va[...], total[0:16, :])[0]
    row = lax.broadcasted_iota(i32, pn.shape, 0)
    message = jnp.where(row < PIECES, pn, 0.0).astype(bf16)
    for d in range(CHIPS):
        send[d] = message


def server_step(got, pa, ma, va):
    return pl.pallas_call(
        step_kernel,
        out_shape=(SDS((CHIPS, 16, PIECE), bf16), kept((32, PIECE))),
        in_specs=[in_vmem()] * 4,
        out_specs=(in_vmem(),) * 2,
        compiler_params=params_for(16),
        name="server_step",
    )(*map(near, (got, pa, ma, va)))


APART = (0, 1, 4, 5, 2, 3, 6, 7)


def state_kernel(
    sums, pa, ma, va, pb, mb, vb, col_0, col_1, pa_n, ma_n, va_n, pb_n, mb_n, vb_n, wide, scr
):
    col = lax.axis_index("x") * 2 + lax.axis_index("zh")
    for n, apart in enumerate(APART):
        block = (col_0, col_1)[n // 4][pl.ds(n % 4 * 8, 8), :]
        owner = jnp.bitwise_xor(col, apart)
        for q in range(3):
            scr[q, owner] = block[2 * q : 2 * q + 2, :]
    grad = sums[16:32, :]
    whole = [scr[q].reshape(RANKS, DEPTH) for q in range(3)]
    full = adaptive_update(*whole, grad)[0]
    k = lax.broadcasted_iota(i32, (RANKS, 256), 1)
    r = lax.broadcasted_iota(i32, (RANKS, 256), 0)
    core = lax.axis_index("c")
    parity = jnp.bitwise_xor(lax.shift_right_logical(k, 7), core)
    rank = jnp.bitwise_and(lax.shift_right_logical(k, 4), 7) * 2 + parity
    repeat = jnp.where(rank == r, adapter_scale, 0.0).astype(bf16)
    tall = jnp.transpose(full).astype(bf16)
    wide[...] = jnp.dot(tall, repeat, preferred_element_type=f32).astype(bf16)
    own = [
        jnp.sum(jnp.where(r[:, 0:1] == 2 * col + q, grad, 0.0), axis=0, keepdims=True)
        for q in range(2)
    ]
    pb_n[...], mb_n[...], vb_n[...] = adaptive_update(
        pb[...], mb[...], vb[...], jnp.concatenate(own, axis=0)
    )
    news = adaptive_update(pa[...], ma[...], va[...], sums[0:16, :])
    for ref, new in zip((pa_n, ma_n, va_n), news):
        for i in range(PIECES):
            ref[:, pl.ds(i * PIECE, PIECE)] = new[i : i + 1, :]


def server_state(sums, a_state, b_state, col_state):
    a_shape, b_shape = SDS((1, WIDTH), f32), SDS((2, DEPTH), f32)
    return pl.pallas_call(
        state_kernel,
        out_shape=(a_shape,) * 3 + (b_shape,) * 3 + (kept((DEPTH, 256), bf16),),
        in_specs=[in_vmem()] * 9,
        out_specs=(in_vmem(),) * 7,
        scratch_shapes=[pltpu.VMEM((3, COLS, 2, DEPTH), f32)],
        compiler_params=params_for(16),
        name="server_state",
    )(*map(near, (sums, *a_state, *b_state)), *col_state)


GROUPS = (2, 5, 6)


def merge_kernel(dec_0, dec_1, scale, wide, ranks, mate_ranks, merged, peaks, buf, row_scale, tops, sems):
    fetches, piece = [], 0
    for n, count in enumerate(GROUPS):
        here = pl.ds(piece * PIECE, count * PIECE)
        fetches.append([])
        row = 0
        for q, dec in enumerate((dec_0, dec_1)):
            to = buf.at[pl.ds(row, ROW_PARTS[q]), here]
            fetches[-1].append(pltpu.make_async_copy(dec.at[:, here], to, sems.at[n, q]))
            fetches[-1][-1].start()
            row += ROW_PARTS[q]
        piece += count
    row_scale[...] = jnp.transpose(jnp.broadcast_to(scale[...], (128, DEPTH)))
    lane = jnp.bitwise_and(lax.broadcasted_iota(i32, (DEPTH, 256), 1), 15)
    right = jnp.concatenate([r[...].reshape(128, PIECE) for r in (ranks, mate_ranks)], axis=0)
    tops[...] = jnp.zeros_like(tops)
    piece = 0
    for n, count in enumerate(GROUPS):
        for fetch in fetches[n]:
            fetch.wait()
        for i in range(piece, piece + count):
            one = jnp.where(lane == i, wide[...], jnp.zeros((DEPTH, 256), bf16))
            low = jnp.dot(one, right, preferred_element_type=f32)
            top = tops[...]
            for t in range(PIECE // 128):
                at = t * 128
                code = buf[:, pl.ds(i * PIECE + at, 128)].astype(f32)
                whole = code * row_scale[...] + low[:, at : at + 128]
                merged[i, :, pl.ds(at, 128)] = whole
                top = jnp.maximum(top, jnp.abs(whole))
            tops[...] = top
        piece += count
    peak = jnp.max(jnp.transpose(tops[...]), axis=0, keepdims=True)
    for c in range(COLS):
        peaks[c] = peak


def merge(decs, scale, wide, ranks, mate_ranks):
    return pl.pallas_call(
        merge_kernel,
        out_shape=(pltpu.VMEM((PIECES, DEPTH, PIECE), f32), SDS((COLS, 1, DEPTH), f32)),
        in_specs=[in_hbm()] * 2 + [in_vmem()] * 4,
        out_specs=(in_vmem(), in_vmem()),
        scratch_shapes=[
            pltpu.VMEM((DEPTH, WIDTH), f8),
            pltpu.VMEM((DEPTH, 128), f32),
            pltpu.VMEM((DEPTH, 128), f32),
            pltpu.SemaphoreType.DMA((len(GROUPS), 2)),
        ],
        compiler_params=params_for(20),
        name="merge",
    )(*map(stay, decs), scale, near(wide), near(ranks), near(mate_ranks))


OUT_ROWS = 32


def normalise_kernel(merged, peaks, out, scales, inverse, buf, sems):
    peak = peaks[0]
    for c in range(1, COLS):
        peak = jnp.maximum(peak, peaks[c])
    peak = peak + peak_eps
    scales[...] = peak / fp8_top
    inverse[...] = jnp.transpose(jnp.broadcast_to(1.0 / peak, (128, DEPTH)))
    steps, slots = DEPTH // OUT_ROWS, 8

    def store(step, slot):
        return pltpu.make_async_copy(
            buf.at[slot],
            out.at[pl.ds(pl.multiple_of(step * OUT_ROWS, OUT_ROWS), OUT_ROWS), :],
            sems.at[slot],
        )

    def step(s, carry):
        slot = lax.rem(s, slots)

        @pl.when(s >= slots)
        def _():
            store(s - slots, slot).wait()

        for g in range(OUT_ROWS // 16):
            row = pl.multiple_of(s * OUT_ROWS + g * 16, 16)
            inv = inverse[pl.ds(row, 16), :]
            inv = jnp.concatenate([inv] * (PIECE // 128), axis=1)
            for t in range(PIECES):
                here = pl.ds(t * PIECE, PIECE)
                buf[slot, pl.ds(g * 16, 16), here] = (merged[t, pl.ds(row, 16), :] * inv).astype(bf16)
        store(s, slot).start()
        return carry

    lax.fori_loop(0, steps, step, 0)
    for s in range(steps - slots, steps):
        store(s, s % slots).wait()


def normalise(merged, peaks):
    return pl.pallas_call(
        normalise_kernel,
        out_shape=(SDS((DEPTH, WIDTH), bf16), SDS((1, DEPTH), f32)),
        in_specs=[in_vmem(), in_vmem()],
        out_specs=(in_hbm(), in_vmem()),
        scratch_shapes=[
            pltpu.VMEM((DEPTH, 128), f32),
            pltpu.VMEM((8, OUT_ROWS, WIDTH), bf16),
            pltpu.SemaphoreType.DMA((8,)),
        ],
        compiler_params=params_for(16),
        name="normalise",
    )(near(merged), peaks)


def local(codes, scale, pb, pa, mb, vb, ma, va, delta_b, delta_a, tallies):
    exchange = functools.partial(lax.all_to_all, split_axis=0, concat_axis=0, tiled=True)
    swap = functools.partial(lax.ppermute, perm=[(0, 1), (1, 0)])
    own_a = delta_a.reshape(RANKS, FULL_A)
    own_b = delta_b.reshape(FULL_B, RANKS).T
    mate_a, mate_b, mate_n = swap(own_a, "c"), swap(own_b, "c"), swap(tallies, "c")
    pb, mb, vb = pb.T, mb.T, vb.T
    block = jnp.concatenate([pb, mb, vb, pb], axis=0)
    other = swap(block, "zh")
    own_n, own_a, own_b = own_deltas(tallies, own_a, own_b)
    pairs = pair_sum(own_n, mate_n, own_a, mate_a, own_b, mate_b)
    pairs, codes, block, other = lax.optimization_barrier((pairs, codes, block, other))
    got = exchange(pairs.reshape(CHIPS, 8, LANES), ("zl", "y"))
    for apart in (2, 1):
        block = jnp.concatenate([block, other], axis=0)
        other = lax.ppermute(block, "x", [(k, k ^ apart) for k in range(4)])
    dec_0, *state = decode(codes, 0, ROW_PARTS[0], (pa, ma, va, pb, mb, vb))
    got, dec_0, block, other, state = lax.optimization_barrier((got, dec_0, block, other, state))
    message = row_sum(got)
    codes, message = lax.optimization_barrier((codes, message))
    got = exchange(message, COL)
    (dec_1,) = decode(codes, *ROW_PARTS)
    got, dec_1 = lax.optimization_barrier((got, dec_1))
    send, sums = server_step(got, *state[:3])
    ranks = exchange(send, ("zl", "y"))
    pa_n, ma_n, va_n, pb_n, mb_n, vb_n, wide = server_state(
        sums, state[:3], state[3:], (block, other)
    )
    merged, peaks = merge((dec_0, dec_1), scale.reshape(1, DEPTH), wide, ranks, swap(ranks, "c"))
    out, scales = normalise(merged, exchange(peaks, COL))
    return (out, scales.reshape(DEPTH), pb_n.T, pa_n, mb_n.T, vb_n.T, ma_n, va_n)


def solution(mesh):
    split = Mesh(mesh.devices.reshape(2, 4, 2, 4, 2), ROW + COL)
    tile, everyone = P(ROW, COL), P(ROW + COL, None, None)
    return jax.shard_map(
        local,
        mesh=split,
        in_specs=(tile, P(ROW)) + (tile,) * 6 + (everyone, everyone, P(ROW + COL, None)),
        out_specs=(tile, P(ROW)) + (tile,) * 6,
        check_vma=False,
    )
```
